256 devices in a mesh: path: 16 (over z, core), fsdp: 16 (over y, x).
Axes of the slice: x: 4, y: 4, z: 8, core: 2. Of those that a mesh axis runs over, the one named last changes fastest.
Arguments:
- path_delta: bfloat16 [16, 4, 512, 4096], P('path', None, 'fsdp'), may hold values from -20 to 20
- feedback: float32 [16, 4, 512, 4096], P('path', None, 'fsdp'), may hold values from -4 to 4
- global_params: float32 [4, 2, 512, 4096], P(None, None, 'fsdp', 'path'), may hold values from -0.09375 to 0.09375
- momentum: float32 [4, 2, 512, 4096], P(None, None, 'fsdp', 'path'), may hold values from -2 to 2
- routes: int32 [16, 4], replicated, may hold values from 0 to 1
- token_counts: int32 [16, 4], replicated, may hold values from 1 to 16
- skip_flags: int32 [4, 2], replicated, may hold values from 0 to 1, as said below
Outputs:
- feedback_next: float32 [16, 4, 512, 4096], P('path', None, 'fsdp')
- momentum_next: float32 [4, 2, 512, 4096], P(None, None, 'fsdp', 'path')
- params_next: float32 [4, 2, 512, 4096], P(None, None, 'fsdp', 'path')
- path_params: bfloat16 [16, 4, 512, 4096], P('path', None, 'fsdp')
The draws below stay inside these ranges and needn't reach their ends.
Inputs may be any that keep to these rules, and one draw needn't show every extreme that they name: `skip_flags`: at most one of the two modules of a level skips.
All inputs are finite; a program needn't handle non-finite values.
Results may differ from the reference program's by a relative error of at most 0.012.
Values may be sent and summed in bfloat16 or wider, within the bound.
No kernel may reach another device: no remote copies, remote signals or barrier semaphores. Data moves between devices by JAX's collectives and lax.ppermute only.
A program may use at most 64 MiB of HBM per device.

```python
import jax
import jax.numpy as jnp
from jax import lax

D = 4096
LEVELS = 4
PATHS = 16
PROWS = 512


def level_scale(key):
    quiet = jax.random.randint(jax.random.fold_in(key, 4242), (), 0, LEVELS)
    levels = jnp.arange(LEVELS, dtype=jnp.int32)
    return jnp.where(levels == quiet, 0.05, 1.0).astype(jnp.float32)[None, :, None, None]


def draw_path_delta(key, part):
    first_key = jax.random.fold_in(jax.random.fold_in(key, 17), 0)
    own = jax.random.truncated_normal(first_key, -4.0, 4.0, (PATHS, LEVELS, PROWS, D), jnp.float32)
    rowfrac = jnp.arange(PROWS, dtype=jnp.float32) / max(PROWS - 1, 1)
    colfrac = jnp.arange(D, dtype=jnp.float32) / (D - 1)
    scales = (1.0 + 2.0 * rowfrac)[:, None] * (1.0 + 2.0 * colfrac)[None, :] / 3.0
    mixed = own
    return jnp.clip(level_scale(key) * scales * mixed, -20.0, 20.0).astype(jnp.bfloat16)


def draw_feedback(key, part):
    values = jax.random.truncated_normal(jax.random.fold_in(key, 23), -8.0, 8.0, (PATHS, LEVELS, PROWS, D), jnp.float32)
    return jnp.clip(0.5 * level_scale(key) * values, -4.0, 4.0).astype(jnp.float32)


def draw_skip_flags(key, part):
    pattern = jax.random.randint(jax.random.fold_in(key, 31), (LEVELS,), 0, 3)
    first = (pattern == 0).astype(jnp.int32)
    second = (pattern == 1).astype(jnp.int32)
    return jnp.stack([first, second], axis=1)


def place_ends(drawn, stream_key, low, top_value):
    shape = drawn.shape
    place = [jax.random.randint(jax.random.fold_in(stream_key, axis), (), 0, shape[axis]) for axis in range(len(shape))]
    drawn = drawn.at[tuple(place)].set(low)
    longest = shape.index(max(shape))
    place[longest] = (place[longest] + 1) % shape[longest]
    return drawn.at[tuple(place)].set(top_value)


def block_scale(key, dims, shards, low, largest):
    factor_of, own = 1.0, jax.random.fold_in(key, 6)
    for dim, parts in shards:
        heights = jnp.exp(jax.random.uniform(jax.random.fold_in(own, dim), (parts,), jnp.float32, low / len(shards), largest / len(shards)))
        factor_of = factor_of * jnp.repeat(heights, dims[dim] // parts).reshape([-1 if axis == dim else 1 for axis in range(len(dims))])
    return factor_of


def normal_values(stream_key, shape, deviation, limit, pieces=(), held_as=jnp.bfloat16):
    drawn = jax.random.normal(stream_key, shape, jnp.float32) * deviation
    if len(pieces) > 0:
        drawn = block_scale(stream_key, shape, pieces, -0.22, 0.18) * drawn
    return jnp.clip(drawn, min=-limit, max=limit).astype(held_as)


def setup_inputs(seed: int = 0) -> dict:
    key_list = jax.random.split(jax.random.key(seed), 8)
    return {
        "path_delta": draw_path_delta(jax.random.fold_in(key_list[7], 71), 0),
        "feedback": draw_feedback(jax.random.fold_in(key_list[7], 71), 0),
        "global_params": normal_values(key_list[2], (LEVELS, 2, PROWS, D), D ** -0.5, 0.09375, ((2, 16), (3, 16)), jnp.float32),
        "momentum": normal_values(key_list[3], (LEVELS, 2, PROWS, D), 0.3, 2.0, ((2, 16), (3, 16)), jnp.float32),
        "routes": place_ends(jax.random.randint(key_list[4], (PATHS, LEVELS), 0, 2), jax.random.fold_in(key_list[4], 1), 0, 1).astype(jnp.int32),
        "token_counts": place_ends(jax.random.randint(key_list[5], (PATHS, LEVELS), 1, 17), jax.random.fold_in(key_list[5], 1), 1, 16).astype(jnp.int32),
        "skip_flags": draw_skip_flags(jax.random.fold_in(key_list[7], 71), 0),
    }


clip_rms = 0.2
outer_rate = 0.7
momentum_coef = 0.9
epsilon_sq = 1e-06

def reference(path_delta, feedback, global_params, momentum, routes, token_counts, skip_flags):
    counts = token_counts.astype(jnp.float32)
    same = (routes[:, None, :] == routes[None, :, :]).astype(jnp.float32)
    denom = lax.optimization_barrier(jnp.sum(same * counts[None, :, :], axis=1))
    weight = counts / denom
    skipped_path = jnp.where(routes == 1, skip_flags[None, :, 1], skip_flags[None, :, 0])
    live = (1 - skipped_path).astype(jnp.float32)
    feedback_parts = []
    average_parts = []
    for level in range(LEVELS):
        corrected = path_delta[:, level].astype(jnp.float32) + feedback[:, level]
        scaled = (weight[:, level, None, None] * corrected).astype(jnp.bfloat16)
        sent = jnp.where(live[:, level, None, None] > 0, scaled, jnp.zeros_like(scaled))
        sent_wide = sent.astype(jnp.float32)
        feedback_parts.append(corrected - live[:, level, None, None] * (sent_wide / weight[:, level, None, None]))
        upper = (routes[:, level] == 1).astype(jnp.float32)
        first = lax.optimization_barrier(jnp.sum((1.0 - upper)[:, None, None] * sent_wide, axis=0))
        second = lax.optimization_barrier(jnp.sum(upper[:, None, None] * sent_wide, axis=0))
        average_parts.append(jnp.stack([first, second]))
    feedback_next = jnp.stack(feedback_parts, axis=1)
    average = jnp.stack(average_parts)
    mean_sq = lax.optimization_barrier(jnp.mean(average * average, axis=(2, 3)))
    factor = jnp.minimum(1.0, clip_rms / jnp.sqrt(mean_sq + epsilon_sq))
    clipped = factor[:, :, None, None] * average
    skipped = (skip_flags > 0)[:, :, None, None]
    momentum_next = jnp.where(skipped, momentum, momentum_coef * momentum + clipped)
    params_next = jnp.where(skipped, global_params, global_params - outer_rate * (clipped + momentum_coef * momentum_next))
    narrow = params_next.astype(jnp.bfloat16)
    returned = []
    for level in range(LEVELS):
        pick = (routes[:, level] == 1)[:, None, None]
        returned.append(jnp.where(pick, narrow[level, 1][None], narrow[level, 0][None]))
    path_params = jnp.stack(returned, axis=1)
    return (feedback_next, momentum_next, params_next, path_params)
```

```python
import jax
import jax.numpy as jnp
from jax import lax
from jax.experimental import pallas as pl
from jax.experimental.pallas import tpu as pltpu
from jax.sharding import Mesh
from jax.sharding import PartitionSpec as P

PATH = ("z", "core")
FSDP = ("y", "x")
PLANE = ("core", "y", "x")
CHIPS = 8
PATHS = 16
LEVELS = 4
SLABS = 8
BLOCK = 256

CLIP_RMS = 0.2
OUTER_RATE = 0.7
MOMENTUM_COEF = 0.9
EPSILON_SQ = 1e-06
CLIPPED_COEF = OUTER_RATE * (1.0 + MOMENTUM_COEF)
MOMENTUM_SHARE = OUTER_RATE * MOMENTUM_COEF * MOMENTUM_COEF

SMEM = pl.BlockSpec(memory_space=pltpu.SMEM)
VMEM = pl.BlockSpec(memory_space=pltpu.VMEM)


def place():
    z, core = lax.axis_index("z"), lax.axis_index("core")
    return z, core, 1 - 2 * core


def chip_at(z, sign, steps):
    return (z + sign * steps) & (CHIPS - 1)


def path_terms(l, routes, counts, flags, rows):
    z, core, _ = place()
    p = 2 * z + core
    own = routes[p, l]
    denom = jnp.int32(0)
    for q in range(PATHS):
        denom += jnp.where(routes[q, l] == own, counts[q, l], 0)
    shape = (rows, BLOCK)
    top = jnp.full(shape, counts[p, l], jnp.int32).astype(jnp.float32)
    bottom = jnp.full(shape, denom, jnp.int32).astype(jnp.float32)
    live = flags[l, own] == 0
    return top, bottom, live


def sent_kernel(routes, counts, flags, delta, feedback, keep, give):
    core = lax.axis_index("core")
    top, bottom, live = path_terms(pl.program_id(0), routes, counts, flags, delta.shape[1])
    weight = jnp.where(live, top / bottom, 0.0)
    for half, out in ((core, keep), (1 - core, give)):
        for block in range(CHIPS):
            at = pl.ds(pl.multiple_of((2 * block + half) * BLOCK, BLOCK), BLOCK)
            corrected = delta[0, :, at].astype(jnp.float32) + feedback[0, :, at]
            out[0, block] = (weight * corrected).astype(jnp.bfloat16)


def feedback_kernel(routes, counts, flags, delta, feedback, out):
    top, bottom, live = path_terms(pl.program_id(0), routes, counts, flags, delta.shape[1])
    weight = top / bottom
    back = jnp.where(live, bottom / top, 0.0)
    for block in range(2 * CHIPS):
        at = pl.ds(block * BLOCK, BLOCK)
        corrected = delta[0, :, at].astype(jnp.float32) + feedback[0, :, at]
        sent = (weight * corrected).astype(jnp.bfloat16).astype(jnp.float32)
        out[0, :, at] = corrected - sent * back


def pair_kernel(routes, flags, keep, got, params, momentum, plus, minus, hold):
    z, core, sign = place()
    own, sibling = 2 * z + core, 2 * z + 1 - core

    def write(out, slot, steps):
        q = chip_at(z, sign, steps)
        l, m = q >> 1, q & 1
        mine = jnp.where(routes[own, l] == m, 1.0, 0.0)
        other = jnp.where(routes[sibling, l] == m, 1.0, 0.0)
        for block in range(CHIPS):
            total = mine * keep[l, block].astype(jnp.float32) + other * got[l, block].astype(jnp.float32)
            out[slot, block] = total.astype(jnp.bfloat16)
        share = jnp.where(flags[l, m] > 0, 0.0, MOMENTUM_SHARE)
        out[slot, CHIPS] = (params[q] - share * momentum[q]).astype(jnp.bfloat16)

    for slot, steps in enumerate((1, -2, 3)):
        write(plus, slot, steps)
    for slot, steps in enumerate((-1, -4)):
        write(minus, slot, steps)
    for slot, steps in enumerate((0, -3, 2)):
        write(hold, slot, steps)


def owner_kernel(hold, plus, minus, near, far, average, base, partial):
    z, _, sign = place()
    squares = jnp.zeros(average.shape[1:], jnp.float32)
    for block in range(CHIPS):
        total = hold[0, block].astype(jnp.float32)
        for part in (plus[0, block], minus[0, block], near[block], far[block]):
            total += part.astype(jnp.float32)
        average[block] = total
        squares += total * total
    lanes = jnp.sum(squares, axis=0, keepdims=True)
    lanes = lanes[:, :128] + lanes[:, 128:]
    partial[...] = jnp.broadcast_to(lanes[None], partial.shape)
    for steps, part in (
        (0, hold[0, CHIPS]),
        (-1, plus[0, CHIPS]),
        (1, minus[0, CHIPS]),
        (-2, near[CHIPS]),
        (-3, near[CHIPS + 1]),
        (3, far[CHIPS]),
        (2, far[CHIPS + 1]),
        (4, far[CHIPS + 2]),
    ):
        base[chip_at(z, sign, steps)] = part


def new_kernel(entries, average, base, partials, far, near, own):
    z, _, sign = place()
    total = jnp.sum(jnp.sum(partials[...], axis=0), keepdims=True)
    factor = jnp.minimum(1.0, CLIP_RMS / jnp.sqrt(total / entries + EPSILON_SQ))
    for block in range(CHIPS):
        clipped = factor * average[block]
        new = (base[block].astype(jnp.float32) - CLIPPED_COEF * clipped).astype(jnp.bfloat16)
        far[block] = new
        near[block] = new
        own[block] = new
    for out, jumps in ((far, (3, 4, 2)), (near, (-2, -3)), (own, (0, 1, -1))):
        for slot, steps in enumerate(jumps):
            at = chip_at(z, sign, steps)
            out[CHIPS + slot] = (factor * average[at]).astype(jnp.bfloat16)


def slab_parts(own, near, far, plus, minus):
    return (
        (lambda b: own[b], own.at[CHIPS]),
        (lambda b: minus[0, b], minus.at[0, CHIPS]),
        (lambda b: near[b], near.at[CHIPS]),
        (lambda b: minus[2, b], minus.at[2, CHIPS]),
        (lambda b: plus[1, b], plus.at[1, CHIPS]),
        (lambda b: far[b], far.at[CHIPS]),
        (lambda b: minus[1, b], minus.at[1, CHIPS]),
        (lambda b: plus[0, b], plus.at[0, CHIPS]),
    )


def give_kernel(routes, own, near, far, plus, minus, out):
    z, core, sign = place()
    sibling = 2 * z + 1 - core
    parts = slab_parts(own, near, far, plus, minus)
    for l in range(LEVELS):
        at = ((2 * l + routes[sibling, l] - z) * sign) & (CHIPS - 1)
        for slot, (read, _) in enumerate(parts):

            @pl.when(at == slot)
            def _(l=l, read=read):
                for block in range(CHIPS):
                    out[l, block] = read(block)


def state_kernel(flags, own, near, far, plus, minus, params, momentum, momentum_out, params_out):
    z, _, sign = place()
    parts = slab_parts(own, near, far, plus, minus)
    for slot, (_, ref) in enumerate(parts):
        q = chip_at(z, sign, slot)
        skipped = flags[q >> 1, q & 1] > 0
        clipped = ref[...].astype(jnp.float32)
        before, old = momentum[q], params[q]
        after = jnp.where(skipped, before, MOMENTUM_COEF * before + clipped)
        momentum_out[q] = after
        new = old - OUTER_RATE * (clipped + MOMENTUM_COEF * after)
        params_out[q] = jnp.where(skipped, old, new)


def join_kernel(routes, own, near, far, plus, minus, got, out):
    z, core, sign = place()
    path = 2 * z + core
    parts = slab_parts(own, near, far, plus, minus)
    for l in range(LEVELS):
        at = ((2 * l + routes[path, l] - z) * sign) & (CHIPS - 1)
        for slot, (read, _) in enumerate(parts):

            @pl.when(at == slot)
            def _(l=l, read=read):
                for block in range(CHIPS):
                    out[l, :, pl.ds(pl.multiple_of((2 * block + core) * BLOCK, BLOCK), BLOCK)] = read(block)

        for block in range(CHIPS):
            out[l, :, pl.ds(pl.multiple_of((2 * block + 1 - core) * BLOCK, BLOCK), BLOCK)] = got[l, block]


def cost(bytes_accessed):
    return pl.CostEstimate(flops=0, bytes_accessed=bytes_accessed, transcendentals=0)


def call(kernel, outs, args, scalars):
    shapes = [jax.ShapeDtypeStruct(s, d) for s, d in outs]
    size = sum(a.size * a.dtype.itemsize for a in args) + sum(s.size * s.dtype.itemsize for s in shapes)
    return pl.pallas_call(
        kernel,
        out_shape=shapes,
        in_specs=[SMEM] * scalars + [VMEM] * (len(args) - scalars),
        out_specs=[VMEM] * len(shapes),
        cost_estimate=cost(size),
        compiler_params=pltpu.CompilerParams(vmem_limit_bytes=24 * 2**20),
    )(*args)


def levelwise(kernel, outs, routes, counts, flags, delta, feedback):
    shapes = [jax.ShapeDtypeStruct(s, d) for s, d in outs]

    def one(shape):
        return pl.BlockSpec((1, *shape[1:]), lambda l: (l, *[0] * (len(shape) - 1)))

    size = delta.size * 6 + sum(s.size * s.dtype.itemsize for s in shapes)
    return pl.pallas_call(
        kernel,
        grid=(LEVELS,),
        out_shape=shapes,
        in_specs=[SMEM] * 3 + [one(delta.shape), one(feedback.shape)],
        out_specs=[one(s.shape) for s in shapes],
        cost_estimate=cost(size),
        compiler_params=pltpu.CompilerParams(vmem_limit_bytes=24 * 2**20),
    )(routes, counts, flags, delta, feedback)


def jump(x, steps):
    def target(p):
        z, core = divmod(p, 2)
        sign = 1 - 2 * core
        return 2 * ((z + sign * steps) % CHIPS) + core

    return lax.ppermute(x, PATH, [(p, target(p)) for p in range(PATHS)])


def swap(x):
    return lax.ppermute(x, "core", [(0, 1), (1, 0)])


def on_device(path_delta, feedback, global_params, momentum, routes, token_counts, skip_flags):
    delta, feedback = path_delta[0], feedback[0]
    rows = delta.shape[1]
    params = global_params.reshape(SLABS, rows, BLOCK)
    momentum = momentum.reshape(SLABS, rows, BLOCK)
    f32, bf16 = jnp.float32, jnp.bfloat16
    half = (LEVELS, CHIPS, rows, BLOCK)

    keep, give = levelwise(sent_kernel, [(half, bf16)] * 2, routes, token_counts, skip_flags, delta, feedback)
    got = swap(give)
    plus, minus, hold = call(
        pair_kernel,
        [((n, CHIPS + 1, rows, BLOCK), bf16) for n in (3, 2, 3)],
        (routes, skip_flags, keep, got, params, momentum),
        2,
    )
    plus = jump(plus, 1)
    minus = jump(minus, -1)
    (feedback_next,) = levelwise(
        feedback_kernel, [(delta.shape, f32)], routes, token_counts, skip_flags, delta, feedback
    )
    near = jnp.concatenate([hold[2, :CHIPS] + plus[2, :CHIPS], hold[2, CHIPS:], plus[2, CHIPS:]])
    near = jump(near, 2)
    far = jnp.concatenate(
        [
            hold[1, :CHIPS] + plus[1, :CHIPS] + minus[1, :CHIPS],
            hold[1, CHIPS:],
            plus[1, CHIPS:],
            minus[1, CHIPS:],
        ]
    )
    far = jump(far, -3)
    plane = lax.axis_size(PLANE)
    average, base, partial = call(
        owner_kernel,
        [((CHIPS, rows, BLOCK), f32), ((CHIPS, rows, BLOCK), bf16), ((plane, 1, 128), f32)],
        (hold, plus, minus, near, far),
        0,
    )
    partials = lax.all_to_all(partial, PLANE, 0, 0)
    entries = rows * lax.axis_size(FSDP) * CHIPS * 2 * BLOCK

    def fresh(*refs):
        new_kernel(entries, *refs)

    far, near, own = call(
        fresh,
        [((CHIPS + n, rows, BLOCK), bf16) for n in (3, 2, 3)],
        (average, base, partials),
        0,
    )
    far = jump(far, 3)
    near = jump(near, -2)
    one = CHIPS + 1
    plus = jnp.stack(
        [
            jnp.concatenate([own[:CHIPS], own[one : one + 1]]),
            jnp.concatenate([far[:CHIPS], far[one : one + 1]]),
        ]
    )
    plus = jump(plus, 1)
    minus = jnp.stack(
        [
            jnp.concatenate([own[:CHIPS], own[one + 1 :]]),
            jnp.concatenate([far[:CHIPS], far[one + 1 :]]),
            jnp.concatenate([near[:CHIPS], near[one:]]),
        ]
    )
    minus = jump(minus, -1)
    slabs = (own, near, far, plus, minus)
    (give,) = call(give_kernel, [(half, bf16)], (routes, *slabs), 1)
    got = swap(give)
    momentum_next, params_next = call(
        state_kernel, [(params.shape, f32)] * 2, (skip_flags, *slabs, params, momentum), 1
    )
    (path_params,) = call(join_kernel, [(delta.shape, bf16)], (routes, *slabs, got), 1)
    shape = global_params.shape
    return feedback_next[None], momentum_next.reshape(shape), params_next.reshape(shape), path_params[None]


def solution(mesh):
    finer = Mesh(mesh.devices.reshape(8, 2, 4, 4), (*PATH, *FSDP))
    by_path, by_column = P(PATH, None, FSDP, None), P(None, None, FSDP, PATH)
    return jax.shard_map(
        on_device,
        mesh=finer,
        in_specs=(by_path, by_path, by_column, by_column, P(), P(), P()),
        out_specs=(by_path, by_column, by_column, by_path),
        check_vma=False,
    )
```

```python
import jax
import jax.numpy as jnp
from jax import lax
from jax.experimental import pallas as pl
from jax.experimental.pallas import tpu as pltpu
from jax.sharding import Mesh
from jax.sharding import PartitionSpec as P

PATH = ("z", "core")
FSDP = ("y", "x")
CHIPS = 8
PATHS = 16
LEVELS = 4
MODULES = 8
BLOCK = 256

CLIP_RMS = 0.2
OUTER_RATE = 0.7
MOMENTUM_COEF = 0.9
EPSILON_SQ = 1e-06
CLIPPED_COEF = OUTER_RATE * (1.0 + MOMENTUM_COEF)
MOMENTUM_SHARE = OUTER_RATE * MOMENTUM_COEF * MOMENTUM_COEF

OWN_UPPER, SIBLING_UPPER, SKIPPED, WEIGHT, BACK, TABLE = 0, 4, 8, 16, 20, 24

VMEM = pl.BlockSpec(memory_space=pltpu.VMEM)
HBM = pl.BlockSpec(memory_space=pltpu.HBM)


def place():
    z, core = lax.axis_index("z"), lax.axis_index("core")
    return z, core, 1 - 2 * core


def chip_at(z, sign, steps):
    return (z + sign * steps) & (CHIPS - 1)


def send_half(weight, delta, feedback, half, out):
    for block in range(CHIPS):
        at = pl.ds(pl.multiple_of((2 * block + half) * BLOCK, BLOCK), BLOCK)
        corrected = delta[:, at].astype(jnp.float32) + feedback[:, at]
        out[block] = (weight * corrected).astype(jnp.bfloat16)


def give_kernel(routes_hbm, counts_hbm, flags_hbm, delta, feedback, give, table, *scratch):
    routes, counts, flags, delta_in, feedback_in, sems, table_sems = scratch
    _, rows, _ = delta.shape
    z, core, _ = place()
    path, sibling = 2 * z + core, 2 * z + 1 - core
    small = [
        pltpu.make_async_copy(src, dst, table_sems.at[i])
        for i, (src, dst) in enumerate(((routes_hbm, routes), (counts_hbm, counts), (flags_hbm, flags)))
    ]
    for copy in small:
        copy.start()
    copies = [
        (
            pltpu.make_async_copy(delta.at[l], delta_in.at[l], sems.at[0, l]),
            pltpu.make_async_copy(feedback.at[l], feedback_in.at[l], sems.at[1, l]),
        )
        for l in range(LEVELS)
    ]
    for pair in copies:
        for copy in pair:
            copy.start()
    for copy in small:
        copy.wait()
    tile = table.shape[1:]

    def splat(value):
        return jnp.full(tile, value, jnp.int32).astype(jnp.float32)

    for q in range(MODULES):
        table[SKIPPED + q] = splat(flags[q & 1, q >> 1])
    for l in range(LEVELS):
        own = routes[l, path]
        denom = jnp.int32(0)
        for p in range(PATHS):
            denom += jnp.where(routes[l, p] == own, counts[l, p], 0)
        top, bottom = splat(counts[l, path]), splat(denom)
        ratio = top / bottom
        high = ratio.astype(jnp.bfloat16).astype(jnp.float32)
        rest = (top - high * bottom) - (ratio - high) * bottom
        ratio = ratio + rest / bottom
        live = flags[own, l] == 0
        table[OWN_UPPER + l] = splat(own)
        table[SIBLING_UPPER + l] = splat(routes[l, sibling])
        table[WEIGHT + l] = ratio
        table[BACK + l] = jnp.where(live, bottom / top, 0.0)
        weight = jnp.where(live, ratio, 0.0)[:1]
        for copy in copies[l]:
            copy.wait()
        send_half(weight, delta_in.at[l], feedback_in.at[l], 1 - core, give.at[l])


def keep_kernel(table, delta, feedback, keep):
    core = lax.axis_index("core")
    for l in range(LEVELS):
        weight = jnp.where(table[BACK + l] > 0, table[WEIGHT + l], 0.0)[:1]
        send_half(weight, delta.at[l], feedback.at[l], core, keep.at[l])


def feedback_kernel(table, delta, feedback, out):
    l = pl.program_id(0)
    weight, back = table[WEIGHT + l][:1], table[BACK + l][:1]
    for block in range(2 * CHIPS):
        at = pl.ds(block * BLOCK, BLOCK)
        corrected = delta[0, :, at].astype(jnp.float32) + feedback[0, :, at]
        sent = (weight * corrected).astype(jnp.bfloat16).astype(jnp.float32)
        out[0, :, at] = corrected - sent * back


def write_pairs(table, keep, got, out, jumps):
    z, _, sign = place()
    for l in range(LEVELS):
        own, sibling = table[OWN_UPPER + l][:1], table[SIBLING_UPPER + l][:1]
        for slot, steps in enumerate(jumps):
            chip = chip_at(z, sign, steps)
            first, second = keep[l, chip].astype(jnp.float32), got[l, chip].astype(jnp.float32)
            upper = own * first + sibling * second
            lower = (1.0 - own) * first + (1.0 - sibling) * second
            out[slot, 2 * l] = lower.astype(jnp.bfloat16)
            out[slot, 2 * l + 1] = upper.astype(jnp.bfloat16)


def outgoing_kernel(table, keep, got, plus, minus):
    write_pairs(table, keep, got, plus, (1, -2, 3))
    write_pairs(table, keep, got, minus, (-1, -4))


def staying_kernel(table, keep, got, hold):
    write_pairs(table, keep, got, hold, (0, -3, 2))


def start_kernel(table, params, momentum, start):
    for q in range(MODULES):
        share = MOMENTUM_SHARE * (1.0 - table[SKIPPED + q][:1])
        start[q] = (params[q] - share * momentum[q]).astype(jnp.bfloat16)


def owner_kernel(hold, plus, minus, near, far, average, narrow, partial):
    for q in range(MODULES):
        total = hold[0, q].astype(jnp.float32)
        for part in (plus[0, q], minus[0, q], near[q], far[q]):
            total += part.astype(jnp.float32)
        average[q] = total
        narrow[q] = total.astype(jnp.bfloat16)
        squares = total * total
        squares = squares[:, :128] + squares[:, 128:]
        partial[q : q + 1] = jnp.sum(squares, axis=0, keepdims=True)


def factors(entries, sums):
    total = jnp.sum(sums, axis=1, keepdims=True)
    return jnp.minimum(1.0, CLIP_RMS / jnp.sqrt(total / entries + EPSILON_SQ))


def state_kernel(entries, table, sums, average, params, momentum, momentum_out, params_out):
    factor = factors(entries, jnp.sum(sums[...], axis=0))
    for q in range(MODULES):
        skipped = table[SKIPPED + q][:1] > 0
        clipped = factor[q : q + 1] * average[q]
        before, old = momentum[q], params[q]
        after = jnp.where(skipped, before, MOMENTUM_COEF * before + clipped)
        momentum_out[q] = after
        params_out[q] = jnp.where(skipped, old, old - OUTER_RATE * (clipped + MOMENTUM_COEF * after))


def parts_of(own, near, far, plus, minus):
    return (own, minus.at[0], near, minus.at[2], plus.at[1], far, minus.at[1], plus.at[0])


def new_kernel(entries, row, table, sums, *refs):
    z, _, sign = place()
    *parts, out = refs
    starts, averages = parts_of(*parts[:5]), parts_of(*parts[5:])
    factor = CLIPPED_COEF * factors(entries, jnp.sum(sums[...], axis=0))
    for l in range(LEVELS):
        upper = table[row + l][:1]
        scale_low, scale_high = (1.0 - upper) * factor[2 * l : 2 * l + 1], upper * factor[2 * l + 1 : 2 * l + 2]
        for slot in range(CHIPS):
            start, average = starts[slot], averages[slot]
            base = jnp.where(upper > 0, start[2 * l + 1].astype(jnp.float32), start[2 * l].astype(jnp.float32))
            moved = scale_low * average[2 * l].astype(jnp.float32) + scale_high * average[2 * l + 1].astype(jnp.float32)
            out[l, chip_at(z, sign, slot)] = (base - moved).astype(jnp.bfloat16)


def join_kernel(mine, got, out):
    core = lax.axis_index("core")
    for half, part in ((core, mine), (1 - core, got)):
        for block in range(CHIPS):
            at = pl.ds(pl.multiple_of((2 * block + half) * BLOCK, BLOCK), BLOCK)
            out[0, :, at] = part[0, block]


def cost(bytes_accessed):
    return pl.CostEstimate(flops=0, bytes_accessed=bytes_accessed, transcendentals=0)


def size_of(arrays):
    return sum(a.size * a.dtype.itemsize for a in arrays)


def call(kernel, outs, *args):
    shapes = [jax.ShapeDtypeStruct(s, d) for s, d in outs]
    return pl.pallas_call(
        kernel,
        out_shape=shapes,
        in_specs=[VMEM] * len(args),
        out_specs=[VMEM] * len(shapes),
        cost_estimate=cost(size_of(args) + size_of(shapes)),
        compiler_params=pltpu.CompilerParams(vmem_limit_bytes=24 * 2**20),
    )(*args)


def levelwise(kernel, outs, fixed, *args):
    shapes = [jax.ShapeDtypeStruct(s, d) for s, d in outs]

    def one(shape):
        return pl.BlockSpec((1, *shape[1:]), lambda l: (l, *[0] * (len(shape) - 1)))

    return pl.pallas_call(
        kernel,
        grid=(LEVELS,),
        out_shape=shapes,
        in_specs=[VMEM] * len(fixed) + [one(a.shape) for a in args],
        out_specs=[one(s.shape) for s in shapes],
        cost_estimate=cost(size_of(args) + size_of(shapes)),
        compiler_params=pltpu.CompilerParams(vmem_limit_bytes=24 * 2**20),
    )(*fixed, *args)


def given_half(routes, counts, flags, delta, feedback):
    _, rows, _ = delta.shape
    half = jax.ShapeDtypeStruct((LEVELS, CHIPS, rows, BLOCK), jnp.bfloat16)
    table = jax.ShapeDtypeStruct((TABLE, 8, BLOCK), jnp.float32)
    return pl.pallas_call(
        give_kernel,
        out_shape=[half, table],
        in_specs=[HBM] * 5,
        out_specs=[VMEM] * 2,
        scratch_shapes=[
            pltpu.SMEM(routes.shape, jnp.int32),
            pltpu.SMEM(counts.shape, jnp.int32),
            pltpu.SMEM(flags.shape, jnp.int32),
            pltpu.VMEM(delta.shape, delta.dtype),
            pltpu.VMEM(feedback.shape, feedback.dtype),
            pltpu.SemaphoreType.DMA((2, LEVELS)),
            pltpu.SemaphoreType.DMA((3,)),
        ],
        cost_estimate=cost(half.size * 16),
        compiler_params=pltpu.CompilerParams(vmem_limit_bytes=56 * 2**20),
    )(routes, counts, flags, delta, feedback)


def jump(x, steps):
    def target(p):
        z, core = divmod(p, 2)
        sign = 1 - 2 * core
        return 2 * ((z + sign * steps) % CHIPS) + core

    return lax.ppermute(x, PATH, [(p, target(p)) for p in range(PATHS)])


def swap(x):
    return lax.ppermute(x, "core", [(0, 1), (1, 0)])


def spread_far(x):
    return jump(x, 3), jump(x, -2)


def spread_near(x, far, near):
    plus = jump(jnp.stack([x, far]), 1)
    minus = jump(jnp.stack([x, far, near]), -1)
    return x, near, far, plus, minus


def summed(x, axes):
    parts = jnp.broadcast_to(x[None], (lax.axis_size(axes), *x.shape))
    return lax.all_to_all(parts, axes, 0, 0)


def on_device(path_delta, feedback, global_params, momentum, routes, token_counts, skip_flags):
    delta, feedback = path_delta[0], feedback[0]
    rows = delta.shape[1]
    params = global_params.reshape(MODULES, rows, BLOCK)
    momentum = momentum.reshape(MODULES, rows, BLOCK)
    f32, bf16 = jnp.float32, jnp.bfloat16
    half, block = (LEVELS, CHIPS, rows, BLOCK), (MODULES, rows, BLOCK)
    entries = rows * lax.axis_size(FSDP) * BLOCK * lax.axis_size(PATH)

    give, table = given_half(routes.T, token_counts.T, skip_flags.T, delta, feedback)
    got = swap(give)
    (keep,) = call(keep_kernel, [(half, bf16)], table, delta, feedback)
    plus, minus = call(outgoing_kernel, [((3, *block), bf16), ((2, *block), bf16)], table, keep, got)
    later, _ = lax.optimization_barrier((table, minus))
    plus, minus = jump(plus, 1), jump(minus, -1)
    (start,) = call(start_kernel, [(block, bf16)], later, params, momentum)
    later, _ = lax.optimization_barrier((later, start))
    (hold,) = call(staying_kernel, [((3, *block), bf16)], later, keep, got)
    (feedback_next,) = levelwise(feedback_kernel, [(delta.shape, f32)], (later,), delta, feedback)
    far, near = spread_far(start)
    hold, feedback_next = lax.optimization_barrier((hold, feedback_next))
    reduced_near = jump(hold[2] + plus[2], 2)
    reduced_far = jump(hold[1] + plus[1] + minus[1], -3)
    starts = spread_near(start, far, near)
    average, narrow, partial = call(
        owner_kernel,
        [(block, f32), (block, bf16), ((MODULES, 128), f32)],
        hold,
        plus,
        minus,
        reduced_near,
        reduced_far,
    )
    sums = jnp.sum(summed(partial, FSDP), axis=0)
    far, near = spread_far(narrow)
    narrow, sums = lax.optimization_barrier((narrow, sums))
    averages = spread_near(narrow, far, near)
    sums = summed(sums, PATH)

    def bound(kernel, *values):
        return lambda *refs: kernel(*values, *refs)

    momentum_next, params_next = call(
        bound(state_kernel, entries), [(block, f32)] * 2, table, sums, average, params, momentum
    )
    (give,) = call(
        bound(new_kernel, entries, SIBLING_UPPER), [(half, bf16)], table, sums, *starts, *averages
    )
    got = swap(give)
    (mine,) = call(bound(new_kernel, entries, OWN_UPPER), [(half, bf16)], table, sums, *starts, *averages)
    (path_params,) = levelwise(join_kernel, [(delta.shape, bf16)], (), mine, got)
    shape = global_params.shape
    return feedback_next[None], momentum_next.reshape(shape), params_next.reshape(shape), path_params[None]


def solution(mesh):
    finer = Mesh(mesh.devices.reshape(8, 2, 4, 4), (*PATH, *FSDP))
    by_path, by_column = P(PATH, None, FSDP, None), P(None, None, FSDP, PATH)
    return jax.shard_map(
        on_device,
        mesh=finer,
        in_specs=(by_path, by_path, by_column, by_column, P(), P(), P()),
        out_specs=(by_path, by_column, by_column, by_path),
        check_vma=False,
    )
```

```python
import jax
import jax.numpy as jnp
from jax import lax
from jax.experimental import pallas as pl
from jax.experimental.pallas import tpu as pltpu
from jax.sharding import Mesh
from jax.sharding import PartitionSpec as P

PATH = ("z", "core")
FSDP = ("y", "x")
CHIPS = 8
PATHS = 16
LEVELS = 4
MODULES = 8
BLOCK = 256

CLIP_RMS = 0.2
OUTER_RATE = 0.7
MOMENTUM_COEF = 0.9
EPSILON_SQ = 1e-06
CLIPPED_COEF = OUTER_RATE * (1.0 + MOMENTUM_COEF)
MOMENTUM_SHARE = OUTER_RATE * MOMENTUM_COEF * MOMENTUM_COEF

OWN_UPPER, SIBLING_UPPER, SKIPPED, WEIGHT, BACK, TABLE = 0, 4, 8, 16, 20, 24

VMEM = pl.BlockSpec(memory_space=pltpu.VMEM)
HBM = pl.BlockSpec(memory_space=pltpu.HBM)


def place():
    z, core = lax.axis_index("z"), lax.axis_index("core")
    return z, core, 1 - 2 * core


def chip_at(z, sign, steps):
    return (z + sign * steps) & (CHIPS - 1)


def send_half(weight, delta, feedback, half, out):
    for block in range(CHIPS):
        at = pl.ds(pl.multiple_of((2 * block + half) * BLOCK, BLOCK), BLOCK)
        corrected = delta[:, at].astype(jnp.float32) + feedback[:, at]
        out[block] = (weight * corrected).astype(jnp.bfloat16)


def give_kernel(routes_hbm, counts_hbm, flags_hbm, delta, feedback, give, table, *scratch):
    routes, counts, flags, delta_in, feedback_in, sems, table_sems = scratch
    _, rows, _ = delta.shape
    z, core, _ = place()
    path, sibling = 2 * z + core, 2 * z + 1 - core
    small = [
        pltpu.make_async_copy(src, dst, table_sems.at[i])
        for i, (src, dst) in enumerate(((routes_hbm, routes), (counts_hbm, counts), (flags_hbm, flags)))
    ]
    for copy in small:
        copy.start()
    copies = [
        (
            pltpu.make_async_copy(delta.at[l], delta_in.at[l], sems.at[0, l]),
            pltpu.make_async_copy(feedback.at[l], feedback_in.at[l], sems.at[1, l]),
        )
        for l in range(LEVELS)
    ]
    for pair in copies:
        for copy in pair:
            copy.start()
    for copy in small:
        copy.wait()
    tile = table.shape[1:]

    def splat(value):
        return jnp.full(tile, value, jnp.int32).astype(jnp.float32)

    for q in range(MODULES):
        table[SKIPPED + q] = splat(flags[q & 1, q >> 1])
    for l in range(LEVELS):
        own = routes[l, path]
        denom = jnp.int32(0)
        for p in range(PATHS):
            denom += jnp.where(routes[l, p] == own, counts[l, p], 0)
        top, bottom = splat(counts[l, path]), splat(denom)
        ratio = top / bottom
        high = ratio.astype(jnp.bfloat16).astype(jnp.float32)
        rest = (top - high * bottom) - (ratio - high) * bottom
        ratio = ratio + rest / bottom
        live = flags[own, l] == 0
        table[OWN_UPPER + l] = splat(own)
        table[SIBLING_UPPER + l] = splat(routes[l, sibling])
        table[WEIGHT + l] = ratio
        table[BACK + l] = jnp.where(live, bottom / top, 0.0)
        weight = jnp.where(live, ratio, 0.0)[:1]
        for copy in copies[l]:
            copy.wait()
        send_half(weight, delta_in.at[l], feedback_in.at[l], 1 - core, give.at[l])


def keep_kernel(table, delta, feedback, keep):
    core = lax.axis_index("core")
    for l in range(LEVELS):
        weight = jnp.where(table[BACK + l] > 0, table[WEIGHT + l], 0.0)[:1]
        send_half(weight, delta.at[l], feedback.at[l], core, keep.at[l])


def feedback_kernel(table, delta, feedback, out):
    l = pl.program_id(0)
    weight, back = table[WEIGHT + l][:1], table[BACK + l][:1]
    for block in range(2 * CHIPS):
        at = pl.ds(block * BLOCK, BLOCK)
        corrected = delta[0, :, at].astype(jnp.float32) + feedback[0, :, at]
        sent = (weight * corrected).astype(jnp.bfloat16).astype(jnp.float32)
        out[0, :, at] = corrected - sent * back


def write_pairs(table, keep, got, out, jumps):
    z, _, sign = place()
    for l in range(LEVELS):
        own, sibling = table[OWN_UPPER + l][:1], table[SIBLING_UPPER + l][:1]
        for slot, steps in enumerate(jumps):
            chip = chip_at(z, sign, steps)
            first, second = keep[l, chip].astype(jnp.float32), got[l, chip].astype(jnp.float32)
            upper = own * first + sibling * second
            lower = (1.0 - own) * first + (1.0 - sibling) * second
            out[slot, 2 * l] = lower.astype(jnp.bfloat16)
            out[slot, 2 * l + 1] = upper.astype(jnp.bfloat16)


def outgoing_kernel(table, keep, got, plus, minus):
    write_pairs(table, keep, got, plus, (1, -2, 3))
    write_pairs(table, keep, got, minus, (-1, -4))


def staying_kernel(table, keep, got, hold):
    write_pairs(table, keep, got, hold, (0, -3, 2))


def start_kernel(table, params, momentum, start):
    for q in range(MODULES):
        share = MOMENTUM_SHARE * (1.0 - table[SKIPPED + q][:1])
        start[q] = (params[q] - share * momentum[q]).astype(jnp.bfloat16)


def owner_kernel(hold, plus, minus, near, far, average, narrow):
    for q in range(MODULES):
        total = hold[0, q].astype(jnp.float32)
        for part in (plus[0, q], minus[0, q], near[q], far[q]):
            total += part.astype(jnp.float32)
        average[q] = total
        narrow[q] = total.astype(jnp.bfloat16)


def squares_kernel(own, far, near, out):
    lane = lax.broadcasted_iota(jnp.int32, (1, out.shape[1]), 1)
    for q in range(MODULES):
        row = jnp.zeros(lane.shape, jnp.float32)
        for i, block in enumerate((own, far, near)):
            value = block[q].astype(jnp.float32)
            total = jnp.sum(jnp.sum(value * value, axis=0, keepdims=True), axis=1, keepdims=True)
            row = jnp.where(lane == i, total, row)
        out[q : q + 1] = row


def second_kernel(own, far, near, plus, minus):
    for q in range(MODULES):
        plus[q] = own[q]
        plus[MODULES + q] = far[q]
        minus[q] = own[q]
        minus[MODULES + q] = far[q]
        minus[2 * MODULES + q] = near[q]


def parts_of(own, near, far, plus, minus):
    def piece(ref, at):
        return ref.at[pl.ds(at * MODULES, MODULES)]

    return (own, piece(minus, 0), near, piece(minus, 2), piece(plus, 1), far, piece(minus, 1), piece(plus, 0))


def select(row, table, parts, out):
    z, _, sign = place()
    for which in range(2):
        for slot, part in enumerate(parts_of(*parts[5 * which : 5 * which + 5])):
            chip = chip_at(z, sign, slot)
            for l in range(LEVELS):
                upper = table[row + l][:1]
                value = jnp.where(upper > 0, part[2 * l + 1].astype(jnp.float32), part[2 * l].astype(jnp.float32))
                out[which, l, chip] = value.astype(jnp.bfloat16)


def select_kernel(row, table, *refs):
    *parts, out = refs
    select(row, table, parts, out)


def last_kernel(entries, table, sums, other_sums, mine, got, average, params, momentum, path_out, momentum_out, params_out):
    l = pl.program_id(0)
    core = lax.axis_index("core")
    total = jnp.sum(sums[...] + other_sums[...], axis=1, keepdims=True)
    factor = jnp.minimum(1.0, CLIP_RMS / jnp.sqrt(total / entries + EPSILON_SQ))
    row = lax.broadcasted_iota(jnp.int32, factor.shape, 0)
    low, high = (jnp.sum(jnp.where(row == 2 * l + m, factor, 0.0), axis=0, keepdims=True) for m in range(2))
    for m, scale in enumerate((low, high)):
        skipped = table[SKIPPED + 2 * l + m][:1] > 0
        clipped = scale * average[m]
        before, old = momentum[m], params[m]
        after = jnp.where(skipped, before, MOMENTUM_COEF * before + clipped)
        momentum_out[m] = after
        params_out[m] = jnp.where(skipped, old, old - OUTER_RATE * (clipped + MOMENTUM_COEF * after))
    upper = table[OWN_UPPER + l][:1] > 0
    scale = CLIPPED_COEF * jnp.where(upper, high, low)
    for half, part in ((core, mine), (1 - core, got)):
        for block in range(CHIPS):
            at = pl.ds(pl.multiple_of((2 * block + half) * BLOCK, BLOCK), BLOCK)
            new = part[0, l, block].astype(jnp.float32) - scale * part[1, l, block].astype(jnp.float32)
            path_out[0, :, at] = new.astype(jnp.bfloat16)


def cost(bytes_accessed):
    return pl.CostEstimate(flops=0, bytes_accessed=bytes_accessed, transcendentals=0)


def size_of(arrays):
    return sum(a.size * a.dtype.itemsize for a in arrays)


def call(kernel, outs, *args):
    shapes = [jax.ShapeDtypeStruct(s, d) for s, d in outs]
    return pl.pallas_call(
        kernel,
        out_shape=shapes,
        in_specs=[VMEM] * len(args),
        out_specs=[VMEM] * len(shapes),
        cost_estimate=cost(size_of(args) + size_of(shapes)),
        compiler_params=pltpu.CompilerParams(vmem_limit_bytes=24 * 2**20),
    )(*args)


def levelwise(kernel, outs, fixed, *args):
    shapes = [jax.ShapeDtypeStruct(s, d) for s, d in outs]

    def one(shape):
        return pl.BlockSpec((shape[0] // LEVELS, *shape[1:]), lambda l: (l, *[0] * (len(shape) - 1)))

    return pl.pallas_call(
        kernel,
        grid=(LEVELS,),
        out_shape=shapes,
        in_specs=[VMEM] * len(fixed) + [one(a.shape) for a in args],
        out_specs=[one(s.shape) for s in shapes],
        cost_estimate=cost(size_of(args) + size_of(shapes)),
        compiler_params=pltpu.CompilerParams(vmem_limit_bytes=24 * 2**20),
    )(*fixed, *args)


def last(entries, table, sums, other_sums, mine, got, average, params, momentum):
    _, _, _, rows, _ = mine.shape
    outs = [
        jax.ShapeDtypeStruct((LEVELS, rows, 2 * CHIPS * BLOCK), jnp.bfloat16),
        *[jax.ShapeDtypeStruct(average.shape, jnp.float32)] * 2,
    ]

    def one(shape):
        return pl.BlockSpec((shape[0] // LEVELS, *shape[1:]), lambda l: (l, *[0] * (len(shape) - 1)))

    return pl.pallas_call(
        lambda *refs: last_kernel(entries, *refs),
        grid=(LEVELS,),
        out_shape=outs,
        in_specs=[
            VMEM,
            VMEM,
            VMEM,
            VMEM,
            VMEM,
            *[one(average.shape)] * 3,
        ],
        out_specs=[one(o.shape) for o in outs],
        cost_estimate=cost(size_of((mine, got, average, params, momentum)) + size_of(outs)),
        compiler_params=pltpu.CompilerParams(vmem_limit_bytes=24 * 2**20),
    )(table, sums, other_sums, mine, got, average, params, momentum)


def given_half(routes, counts, flags, delta, feedback):
    _, rows, _ = delta.shape
    half = jax.ShapeDtypeStruct((LEVELS, CHIPS, rows, BLOCK), jnp.bfloat16)
    table = jax.ShapeDtypeStruct((TABLE, 8, BLOCK), jnp.float32)
    return pl.pallas_call(
        give_kernel,
        out_shape=[half, table],
        in_specs=[HBM] * 5,
        out_specs=[VMEM] * 2,
        scratch_shapes=[
            pltpu.SMEM(routes.shape, jnp.int32),
            pltpu.SMEM(counts.shape, jnp.int32),
            pltpu.SMEM(flags.shape, jnp.int32),
            pltpu.VMEM(delta.shape, delta.dtype),
            pltpu.VMEM(feedback.shape, feedback.dtype),
            pltpu.SemaphoreType.DMA((2, LEVELS)),
            pltpu.SemaphoreType.DMA((3,)),
        ],
        cost_estimate=cost(half.size * 16),
        compiler_params=pltpu.CompilerParams(vmem_limit_bytes=56 * 2**20),
    )(routes, counts, flags, delta, feedback)


def moved(x, up, down):
    def target(p):
        z, core = divmod(p, 2)
        return 2 * ((z + (down if core else up)) % CHIPS) + core

    return lax.ppermute(x, PATH, [(p, target(p)) for p in range(PATHS)])


def jump(x, steps):
    return moved(x, steps, -steps)


def swap(x):
    return lax.ppermute(x, "core", [(0, 1), (1, 0)])


def spread_far(x):
    return jump(x, 3), jump(x, -2)


def spread_near(x, far, near):
    _, *tile = x.shape
    plus, minus = call(second_kernel, [((n * MODULES, *tile), x.dtype) for n in (2, 3)], x, far, near)
    return x, near, far, jump(plus, 1), jump(minus, -1)


def over_plane(x):
    parts = jnp.broadcast_to(x[None], (lax.axis_size(FSDP), *x.shape))
    return jnp.sum(lax.all_to_all(parts, FSDP, 0, 0), axis=0)


def on_device(path_delta, feedback, global_params, momentum, routes, token_counts, skip_flags):
    delta, feedback = path_delta[0], feedback[0]
    rows = delta.shape[1]
    params = global_params.reshape(MODULES, rows, BLOCK)
    momentum = momentum.reshape(MODULES, rows, BLOCK)
    f32, bf16 = jnp.float32, jnp.bfloat16
    half, block = (LEVELS, CHIPS, rows, BLOCK), (MODULES, rows, BLOCK)
    entries = rows * lax.axis_size(FSDP) * BLOCK * lax.axis_size(PATH)

    give, table = given_half(routes.T, token_counts.T, skip_flags.T, delta, feedback)
    got = swap(give)
    (keep,) = call(keep_kernel, [(half, bf16)], table, delta, feedback)
    plus, minus = call(outgoing_kernel, [((3, *block), bf16), ((2, *block), bf16)], table, keep, got)
    later, _ = lax.optimization_barrier((table, minus))
    plus, minus = jump(plus, 1), jump(minus, -1)
    (start,) = call(start_kernel, [(block, bf16)], later, params, momentum)
    later, _ = lax.optimization_barrier((later, start))
    (hold,) = call(staying_kernel, [((3, *block), bf16)], later, keep, got)
    (feedback_next,) = levelwise(feedback_kernel, [(delta.shape, f32)], (later,), delta, feedback)
    far, near = spread_far(start)
    hold, feedback_next = lax.optimization_barrier((hold, feedback_next))
    reduced_near = jump(hold[2] + plus[2], 2)
    reduced_far = jump(hold[1] + plus[1] + minus[1], -3)
    starts = spread_near(start, far, near)
    average, narrow = call(
        owner_kernel,
        [(block, f32), (block, bf16)],
        hold,
        plus,
        minus,
        reduced_near,
        reduced_far,
    )
    far, near = spread_far(narrow)
    averages = spread_near(narrow, far, near)
    (squares,) = call(squares_kernel, [((MODULES, 128), f32)], narrow, far, near)
    sums = over_plane(squares)
    later, sums = lax.optimization_barrier((table, sums))
    lane = lax.broadcasted_iota(jnp.int32, sums.shape, 1)
    sums = sums + jump(jnp.where(lane < 2, sums, 0.0), 1) + jump(sums, -1)
    other_sums = swap(sums)

    def bound(kernel, value):
        return lambda *refs: kernel(value, *refs)

    chosen = [((2, *half), bf16)]
    (give,) = call(bound(select_kernel, SIBLING_UPPER), chosen, later, *starts, *averages)
    got = swap(give)
    (mine,) = call(bound(select_kernel, OWN_UPPER), chosen, later, *starts, *averages)
    path_params, momentum_next, params_next = last(
        entries, table, sums, other_sums, mine, got, average, params, momentum
    )
    shape = global_params.shape
    return feedback_next[None], momentum_next.reshape(shape), params_next.reshape(shape), path_params[None]


def solution(mesh):
    finer = Mesh(mesh.devices.reshape(8, 2, 4, 4), (*PATH, *FSDP))
    by_path, by_column = P(PATH, None, FSDP, None), P(None, None, FSDP, PATH)
    return jax.shard_map(
        on_device,
        mesh=finer,
        in_specs=(by_path, by_path, by_column, by_column, P(), P(), P()),
        out_specs=(by_path, by_column, by_column, by_path),
        check_vma=False,
    )
```

```python
import jax
import jax.numpy as jnp
from jax import lax
from jax.experimental import pallas as pl
from jax.experimental.pallas import tpu as pltpu
from jax.sharding import Mesh
from jax.sharding import PartitionSpec as P

PATH = ("z", "core")
FSDP = ("y", "x")
CHIPS = 8
PATHS = 16
LEVELS = 4
MODULES = 8
BLOCK = 256

CLIP_RMS = 0.2
OUTER_RATE = 0.7
MOMENTUM_COEF = 0.9
EPSILON_SQ = 1e-06
CLIPPED_COEF = OUTER_RATE * (1.0 + MOMENTUM_COEF)
MOMENTUM_SHARE = OUTER_RATE * MOMENTUM_COEF * MOMENTUM_COEF

OWN_UPPER, SIBLING_UPPER, SKIPPED, WEIGHT, BACK, TABLE = 0, 4, 8, 16, 20, 24

VMEM = pl.BlockSpec(memory_space=pltpu.VMEM)
HBM = pl.BlockSpec(memory_space=pltpu.HBM)


def place():
    z, core = lax.axis_index("z"), lax.axis_index("core")
    return z, core, 1 - 2 * core


def chip_at(z, sign, steps):
    return (z + sign * steps) & (CHIPS - 1)


def send_half(weight, delta, feedback, half, out):
    for block in range(CHIPS):
        at = pl.ds(pl.multiple_of((2 * block + half) * BLOCK, BLOCK), BLOCK)
        corrected = delta[:, at].astype(jnp.float32) + feedback[:, at]
        out[block] = (weight * corrected).astype(jnp.bfloat16)


def give_kernel(routes_hbm, counts_hbm, flags_hbm, delta, feedback, give, table, *scratch):
    routes, counts, flags, delta_in, feedback_in, sems, table_sems = scratch
    _, rows, _ = delta.shape
    z, core, _ = place()
    path, sibling = 2 * z + core, 2 * z + 1 - core
    small = [
        pltpu.make_async_copy(src, dst, table_sems.at[i])
        for i, (src, dst) in enumerate(((routes_hbm, routes), (counts_hbm, counts), (flags_hbm, flags)))
    ]
    for copy in small:
        copy.start()
    copies = [
        (
            pltpu.make_async_copy(delta.at[l], delta_in.at[l], sems.at[0, l]),
            pltpu.make_async_copy(feedback.at[l], feedback_in.at[l], sems.at[1, l]),
        )
        for l in range(LEVELS)
    ]
    for pair in copies:
        for copy in pair:
            copy.start()
    for copy in small:
        copy.wait()
    tile = table.shape[1:]

    def splat(value):
        return jnp.full(tile, value, jnp.int32).astype(jnp.float32)

    for q in range(MODULES):
        table[SKIPPED + q] = splat(flags[q & 1, q >> 1])
    for l in range(LEVELS):
        own = routes[l, path]
        denom = jnp.int32(0)
        for p in range(PATHS):
            denom += jnp.where(routes[l, p] == own, counts[l, p], 0)
        top, bottom = splat(counts[l, path]), splat(denom)
        ratio = top / bottom
        high = ratio.astype(jnp.bfloat16).astype(jnp.float32)
        rest = (top - high * bottom) - (ratio - high) * bottom
        ratio = ratio + rest / bottom
        live = flags[own, l] == 0
        table[OWN_UPPER + l] = splat(own)
        table[SIBLING_UPPER + l] = splat(routes[l, sibling])
        table[WEIGHT + l] = ratio
        table[BACK + l] = jnp.where(live, bottom / top, 0.0)
        weight = jnp.where(live, ratio, 0.0)[:1]
        for copy in copies[l]:
            copy.wait()
        send_half(weight, delta_in.at[l], feedback_in.at[l], 1 - core, give.at[l])


def keep_kernel(table, delta, feedback, keep):
    core = lax.axis_index("core")
    for l in range(LEVELS):
        weight = jnp.where(table[BACK + l] > 0, table[WEIGHT + l], 0.0)[:1]
        send_half(weight, delta.at[l], feedback.at[l], core, keep.at[l])


def feedback_kernel(table, delta, feedback, out):
    l = pl.program_id(0)
    weight, back = table[WEIGHT + l][:1], table[BACK + l][:1]
    for block in range(2 * CHIPS):
        at = pl.ds(block * BLOCK, BLOCK)
        corrected = delta[0, :, at].astype(jnp.float32) + feedback[0, :, at]
        sent = (weight * corrected).astype(jnp.bfloat16).astype(jnp.float32)
        out[0, :, at] = corrected - sent * back


def write_pairs(table, keep, got, out, jumps):
    z, _, sign = place()
    for l in range(LEVELS):
        own, sibling = table[OWN_UPPER + l][:1], table[SIBLING_UPPER + l][:1]
        for slot, steps in enumerate(jumps):
            chip = chip_at(z, sign, steps)
            first, second = keep[l, chip].astype(jnp.float32), got[l, chip].astype(jnp.float32)
            upper = own * first + sibling * second
            lower = (1.0 - own) * first + (1.0 - sibling) * second
            out[slot, 2 * l] = lower.astype(jnp.bfloat16)
            out[slot, 2 * l + 1] = upper.astype(jnp.bfloat16)


def outgoing_kernel(table, keep, got, plus, minus):
    write_pairs(table, keep, got, plus, (1, -2, 3))
    write_pairs(table, keep, got, minus, (-1, -4))


def staying_kernel(table, keep, got, hold):
    write_pairs(table, keep, got, hold, (0, -3, 2))


def start_kernel(table, params, momentum, start):
    for q in range(MODULES):
        share = MOMENTUM_SHARE * (1.0 - table[SKIPPED + q][:1])
        start[q] = (params[q] - share * momentum[q]).astype(jnp.bfloat16)


def owner_kernel(hold, plus, minus, near, far, average, narrow):
    for q in range(MODULES):
        total = hold[0, q].astype(jnp.float32)
        for part in (plus[0, q], minus[0, q], near[q], far[q]):
            total += part.astype(jnp.float32)
        average[q] = total
        narrow[q] = total.astype(jnp.bfloat16)


def squares_kernel(own, far, near, out):
    lane = lax.broadcasted_iota(jnp.int32, (1, out.shape[1]), 1)
    for q in range(MODULES):
        row = jnp.zeros(lane.shape, jnp.float32)
        for i, block in enumerate((own, far, near)):
            value = block[q].astype(jnp.float32)
            total = jnp.sum(jnp.sum(value * value, axis=0, keepdims=True), axis=1, keepdims=True)
            row = jnp.where(lane == i, total, row)
        out[q : q + 1] = row


def second_kernel(*refs):
    *blocks, plus, minus = refs
    for i, block in enumerate(blocks):
        which, kind = divmod(i, 3)
        for q in range(MODULES):
            value = block[q]
            minus[(3 * which + kind) * MODULES + q] = value
            if kind < 2:
                plus[(2 * which + kind) * MODULES + q] = value


def parts_of(which, own, far, near, plus, minus):
    def above(at):
        return plus.at[pl.ds((2 * which + at) * MODULES, MODULES)]

    def below(at):
        return minus.at[pl.ds((3 * which + at) * MODULES, MODULES)]

    return (own, below(0), near, below(2), above(1), far, below(1), above(0))


def select_kernel(row, table, *refs):
    z, _, sign = place()
    *blocks, plus, minus, out = refs
    for which in range(2):
        parts = parts_of(which, *blocks[3 * which : 3 * which + 3], plus, minus)
        for slot, part in enumerate(parts):
            chip = chip_at(z, sign, slot)
            for l in range(LEVELS):
                upper = table[row + l][:1]
                value = jnp.where(upper > 0, part[2 * l + 1].astype(jnp.float32), part[2 * l].astype(jnp.float32))
                out[which, l, chip] = value.astype(jnp.bfloat16)


def last_kernel(entries, table, sums, other_sums, mine, got, average, params, momentum, path_out, momentum_out, params_out):
    l = pl.program_id(0)
    core = lax.axis_index("core")
    total = jnp.sum(sums[...] + other_sums[...], axis=1, keepdims=True)
    factor = jnp.minimum(1.0, CLIP_RMS / jnp.sqrt(total / entries + EPSILON_SQ))
    row = lax.broadcasted_iota(jnp.int32, factor.shape, 0)
    low, high = (jnp.sum(jnp.where(row == 2 * l + m, factor, 0.0), axis=0, keepdims=True) for m in range(2))
    for m, scale in enumerate((low, high)):
        skipped = table[SKIPPED + 2 * l + m][:1] > 0
        clipped = scale * average[m]
        before, old = momentum[m], params[m]
        after = jnp.where(skipped, before, MOMENTUM_COEF * before + clipped)
        momentum_out[m] = after
        params_out[m] = jnp.where(skipped, old, old - OUTER_RATE * (clipped + MOMENTUM_COEF * after))
    upper = table[OWN_UPPER + l][:1] > 0
    scale = CLIPPED_COEF * jnp.where(upper, high, low)
    for half, part in ((core, mine), (1 - core, got)):
        for block in range(CHIPS):
            at = pl.ds(pl.multiple_of((2 * block + half) * BLOCK, BLOCK), BLOCK)
            new = part[1, l, block].astype(jnp.float32) - scale * part[0, l, block].astype(jnp.float32)
            path_out[0, :, at] = new.astype(jnp.bfloat16)


def cost(bytes_accessed):
    return pl.CostEstimate(flops=0, bytes_accessed=bytes_accessed, transcendentals=0)


def size_of(arrays):
    return sum(a.size * a.dtype.itemsize for a in arrays)


def call(kernel, outs, *args):
    shapes = [jax.ShapeDtypeStruct(s, d) for s, d in outs]
    return pl.pallas_call(
        kernel,
        out_shape=shapes,
        in_specs=[VMEM] * len(args),
        out_specs=[VMEM] * len(shapes),
        cost_estimate=cost(size_of(args) + size_of(shapes)),
        compiler_params=pltpu.CompilerParams(vmem_limit_bytes=24 * 2**20),
    )(*args)


def levelwise(kernel, outs, fixed, *args):
    shapes = [jax.ShapeDtypeStruct(s, d) for s, d in outs]

    def one(shape):
        return pl.BlockSpec((shape[0] // LEVELS, *shape[1:]), lambda l: (l, *[0] * (len(shape) - 1)))

    return pl.pallas_call(
        kernel,
        grid=(LEVELS,),
        out_shape=shapes,
        in_specs=[VMEM] * len(fixed) + [one(a.shape) for a in args],
        out_specs=[one(s.shape) for s in shapes],
        cost_estimate=cost(size_of(args) + size_of(shapes)),
        compiler_params=pltpu.CompilerParams(vmem_limit_bytes=24 * 2**20),
    )(*fixed, *args)


def last(entries, table, sums, other_sums, mine, got, average, params, momentum):
    _, _, _, rows, _ = mine.shape
    outs = [
        jax.ShapeDtypeStruct((LEVELS, rows, 2 * CHIPS * BLOCK), jnp.bfloat16),
        *[jax.ShapeDtypeStruct(average.shape, jnp.float32)] * 2,
    ]

    def one(shape):
        return pl.BlockSpec((shape[0] // LEVELS, *shape[1:]), lambda l: (l, *[0] * (len(shape) - 1)))

    return pl.pallas_call(
        lambda *refs: last_kernel(entries, *refs),
        grid=(LEVELS,),
        out_shape=outs,
        in_specs=[
            VMEM,
            VMEM,
            VMEM,
            VMEM,
            VMEM,
            *[one(average.shape)] * 3,
        ],
        out_specs=[one(o.shape) for o in outs],
        cost_estimate=cost(size_of((mine, got, average, params, momentum)) + size_of(outs)),
        compiler_params=pltpu.CompilerParams(vmem_limit_bytes=24 * 2**20),
    )(table, sums, other_sums, mine, got, average, params, momentum)


def given_half(routes, counts, flags, delta, feedback):
    _, rows, _ = delta.shape
    half = jax.ShapeDtypeStruct((LEVELS, CHIPS, rows, BLOCK), jnp.bfloat16)
    table = jax.ShapeDtypeStruct((TABLE, 8, BLOCK), jnp.float32)
    return pl.pallas_call(
        give_kernel,
        out_shape=[half, table],
        in_specs=[HBM] * 5,
        out_specs=[VMEM] * 2,
        scratch_shapes=[
            pltpu.SMEM(routes.shape, jnp.int32),
            pltpu.SMEM(counts.shape, jnp.int32),
            pltpu.SMEM(flags.shape, jnp.int32),
            pltpu.VMEM(delta.shape, delta.dtype),
            pltpu.VMEM(feedback.shape, feedback.dtype),
            pltpu.SemaphoreType.DMA((2, LEVELS)),
            pltpu.SemaphoreType.DMA((3,)),
        ],
        cost_estimate=cost(half.size * 16),
        compiler_params=pltpu.CompilerParams(vmem_limit_bytes=56 * 2**20),
    )(routes, counts, flags, delta, feedback)


def moved(x, up, down):
    def target(p):
        z, core = divmod(p, 2)
        return 2 * ((z + (down if core else up)) % CHIPS) + core

    return lax.ppermute(x, PATH, [(p, target(p)) for p in range(PATHS)])


def jump(x, steps):
    return moved(x, steps, -steps)


def swap(x):
    return lax.ppermute(x, "core", [(0, 1), (1, 0)])


def spread_far(x):
    return jump(x, 3), jump(x, -2)


def spread_near(*blocks):
    _, *tile = blocks[0].shape
    plus, minus = call(second_kernel, [((n * MODULES, *tile), blocks[0].dtype) for n in (4, 6)], *blocks)
    return *blocks, jump(plus, 1), jump(minus, -1)


def over_plane(x):
    parts = jnp.broadcast_to(x[None], (lax.axis_size(FSDP), *x.shape))
    return jnp.sum(lax.all_to_all(parts, FSDP, 0, 0), axis=0)


def on_device(path_delta, feedback, global_params, momentum, routes, token_counts, skip_flags):
    delta, feedback = path_delta[0], feedback[0]
    rows = delta.shape[1]
    params = global_params.reshape(MODULES, rows, BLOCK)
    momentum = momentum.reshape(MODULES, rows, BLOCK)
    f32, bf16 = jnp.float32, jnp.bfloat16
    half, block = (LEVELS, CHIPS, rows, BLOCK), (MODULES, rows, BLOCK)
    entries = rows * lax.axis_size(FSDP) * BLOCK * lax.axis_size(PATH)

    give, table = given_half(routes.T, token_counts.T, skip_flags.T, delta, feedback)
    got = swap(give)
    (keep,) = call(keep_kernel, [(half, bf16)], table, delta, feedback)
    plus, minus = call(outgoing_kernel, [((3, *block), bf16), ((2, *block), bf16)], table, keep, got)
    later, _ = lax.optimization_barrier((table, minus))
    plus, minus = jump(plus, 1), jump(minus, -1)
    (start,) = call(start_kernel, [(block, bf16)], later, params, momentum)
    later, _ = lax.optimization_barrier((later, start))
    (hold,) = call(staying_kernel, [((3, *block), bf16)], later, keep, got)
    (feedback_next,) = levelwise(feedback_kernel, [(delta.shape, f32)], (later,), delta, feedback)
    starts = start, *spread_far(start)
    hold, feedback_next = lax.optimization_barrier((hold, feedback_next))
    reduced_near = jump(hold[2] + plus[2], 2)
    reduced_far = jump(hold[1] + plus[1] + minus[1], -3)
    average, narrow = call(
        owner_kernel,
        [(block, f32), (block, bf16)],
        hold,
        plus,
        minus,
        reduced_near,
        reduced_far,
    )
    far, near = spread_far(narrow)
    spread = spread_near(narrow, far, near, *starts)
    (squares,) = call(squares_kernel, [((MODULES, 128), f32)], narrow, far, near)
    sums = over_plane(squares)
    later, sums = lax.optimization_barrier((table, sums))
    lane = lax.broadcasted_iota(jnp.int32, sums.shape, 1)
    sums = sums + jump(jnp.where(lane < 2, sums, 0.0), 1) + jump(sums, -1)
    other_sums = swap(sums)

    def bound(kernel, value):
        return lambda *refs: kernel(value, *refs)

    chosen = [((2, *half), bf16)]
    (give,) = call(bound(select_kernel, SIBLING_UPPER), chosen, later, *spread)
    got = swap(give)
    (mine,) = call(bound(select_kernel, OWN_UPPER), chosen, later, *spread)
    path_params, momentum_next, params_next = last(
        entries, table, sums, other_sums, mine, got, average, params, momentum
    )
    shape = global_params.shape
    return feedback_next[None], momentum_next.reshape(shape), params_next.reshape(shape), path_params[None]


def solution(mesh):
    finer = Mesh(mesh.devices.reshape(8, 2, 4, 4), (*PATH, *FSDP))
    by_path, by_column = P(PATH, None, FSDP, None), P(None, None, FSDP, PATH)
    return jax.shard_map(
        on_device,
        mesh=finer,
        in_specs=(by_path, by_path, by_column, by_column, P(), P(), P()),
        out_specs=(by_path, by_column, by_column, by_path),
        check_vma=False,
    )
```

```python
import jax
import jax.numpy as jnp
from jax import lax
from jax.experimental import pallas as pl
from jax.experimental.pallas import tpu as pltpu
from jax.sharding import Mesh
from jax.sharding import PartitionSpec as P

PATH = ("z", "core")
FSDP = ("y", "x")
PLANE = ("core", "y", "x")
CHIPS = 8
PATHS = 16
LEVELS = 4
MODULES = 8
BLOCK = 256
STEPS = 4

CLIP_RMS = 0.2
OUTER_RATE = 0.7
MOMENTUM_COEF = 0.9
EPSILON_SQ = 1e-06
CLIPPED_COEF = OUTER_RATE * (1.0 + MOMENTUM_COEF)
MOMENTUM_SHARE = OUTER_RATE * MOMENTUM_COEF * MOMENTUM_COEF

OWN_UPPER, SIBLING_UPPER, SKIPPED, WEIGHT, BACK, TABLE = 0, 4, 8, 16, 20, 24

VMEM = pl.BlockSpec(memory_space=pltpu.VMEM)
HBM = pl.BlockSpec(memory_space=pltpu.HBM)


def place():
    z, core = lax.axis_index("z"), lax.axis_index("core")
    return z, core, 1 - 2 * core


def chip_at(z, sign, steps):
    return (z + sign * steps) & (CHIPS - 1)


def send_half(weight, delta, feedback, half, out):
    for block in range(CHIPS):
        at = pl.ds(pl.multiple_of((2 * block + half) * BLOCK, BLOCK), BLOCK)
        corrected = delta[:, at].astype(jnp.float32) + feedback[:, at]
        out[block] = (weight * corrected).astype(jnp.bfloat16)


def give_kernel(routes_hbm, counts_hbm, flags_hbm, delta, feedback, give, table, *scratch):
    routes, counts, flags, delta_in, feedback_in, sems, table_sems = scratch
    _, rows, _ = delta.shape
    z, core, _ = place()
    path, sibling = 2 * z + core, 2 * z + 1 - core
    small = [
        pltpu.make_async_copy(src, dst, table_sems.at[i])
        for i, (src, dst) in enumerate(((routes_hbm, routes), (counts_hbm, counts), (flags_hbm, flags)))
    ]
    for copy in small:
        copy.start()
    copies = [
        (
            pltpu.make_async_copy(delta.at[l], delta_in.at[l], sems.at[0, l]),
            pltpu.make_async_copy(feedback.at[l], feedback_in.at[l], sems.at[1, l]),
        )
        for l in range(LEVELS)
    ]
    for pair in copies:
        for copy in pair:
            copy.start()
    for copy in small:
        copy.wait()
    tile = table.shape[1:]

    def splat(value):
        return jnp.full(tile, value, jnp.int32).astype(jnp.float32)

    for q in range(MODULES):
        table[SKIPPED + q] = splat(flags[q & 1, q >> 1])
    for l in range(LEVELS):
        own = routes[l, path]
        denom = jnp.int32(0)
        for p in range(PATHS):
            denom += jnp.where(routes[l, p] == own, counts[l, p], 0)
        top, bottom = splat(counts[l, path]), splat(denom)
        ratio = top / bottom
        high = ratio.astype(jnp.bfloat16).astype(jnp.float32)
        rest = (top - high * bottom) - (ratio - high) * bottom
        ratio = ratio + rest / bottom
        live = flags[own, l] == 0
        table[OWN_UPPER + l] = splat(own)
        table[SIBLING_UPPER + l] = splat(routes[l, sibling])
        table[WEIGHT + l] = ratio
        table[BACK + l] = jnp.where(live, bottom / top, 0.0)
        weight = jnp.where(live, ratio, 0.0)[:1]
        for copy in copies[l]:
            copy.wait()
        send_half(weight, delta_in.at[l], feedback_in.at[l], 1 - core, give.at[l])


def keep_kernel(table, delta, feedback, keep):
    core = lax.axis_index("core")
    for l in range(LEVELS):
        weight = jnp.where(table[BACK + l] > 0, table[WEIGHT + l], 0.0)[:1]
        send_half(weight, delta.at[l], feedback.at[l], core, keep.at[l])


def feedback_kernel(table, delta, feedback, out):
    l = pl.program_id(0)
    weight, back = table[WEIGHT + l][:1], table[BACK + l][:1]
    for block in range(2 * CHIPS):
        at = pl.ds(block * BLOCK, BLOCK)
        corrected = delta[0, :, at].astype(jnp.float32) + feedback[0, :, at]
        sent = (weight * corrected).astype(jnp.bfloat16).astype(jnp.float32)
        out[0, :, at] = corrected - sent * back


def write_pairs(table, keep, got, out, jumps):
    z, _, sign = place()
    for l in range(LEVELS):
        own, sibling = table[OWN_UPPER + l][:1], table[SIBLING_UPPER + l][:1]
        for slot, steps in enumerate(jumps):
            chip = chip_at(z, sign, steps)
            first, second = keep[l, chip].astype(jnp.float32), got[l, chip].astype(jnp.float32)
            upper = own * first + sibling * second
            lower = (1.0 - own) * first + (1.0 - sibling) * second
            out[slot, 2 * l] = lower.astype(jnp.bfloat16)
            out[slot, 2 * l + 1] = upper.astype(jnp.bfloat16)


def outgoing_kernel(table, keep, got, plus, minus):
    write_pairs(table, keep, got, plus, (1, -2, 3))
    write_pairs(table, keep, got, minus, (-1, -4))


def staying_kernel(table, keep, got, hold):
    write_pairs(table, keep, got, hold, (0, -3, 2))


def start_kernel(table, params, momentum, start):
    for q in range(MODULES):
        share = MOMENTUM_SHARE * (1.0 - table[SKIPPED + q][:1])
        start[q] = (params[q] - share * momentum[q]).astype(jnp.bfloat16)


def owner_kernel(hold, plus, minus, near, far, average, narrow):
    for q in range(MODULES):
        total = hold[0, q].astype(jnp.float32)
        for part in (plus[0, q], minus[0, q], near[q], far[q]):
            total += part.astype(jnp.float32)
        average[q] = total
        narrow[q] = total.astype(jnp.bfloat16)


def squares_kernel(own, far, near, out):
    lane = lax.broadcasted_iota(jnp.int32, (1, out.shape[1]), 1) - 3 * lax.axis_index("core")
    for q in range(MODULES):
        row = jnp.zeros(lane.shape, jnp.float32)
        for i, block in enumerate((own, far, near)):
            value = block[q].astype(jnp.float32)
            total = jnp.sum(jnp.sum(value * value, axis=0, keepdims=True), axis=1, keepdims=True)
            row = jnp.where(lane == i, total, row)
        out[q : q + 1] = row


def second_kernel(*refs):
    *blocks, plus, minus = refs
    for i, block in enumerate(blocks):
        which, kind = divmod(i, 3)
        for q in range(MODULES):
            value = block[q]
            minus[(3 * which + kind) * MODULES + q] = value
            if kind < 2:
                plus[(2 * which + kind) * MODULES + q] = value


def parts_of(which, own, far, near, plus, minus):
    def above(at):
        return plus.at[pl.ds((2 * which + at) * MODULES, MODULES)]

    def below(at):
        return minus.at[pl.ds((3 * which + at) * MODULES, MODULES)]

    return (own, below(0), near, below(2), above(1), far, below(1), above(0))


def select_kernel(row, table, *refs):
    z, _, sign = place()
    *blocks, plus, minus, out = refs
    for which in range(2):
        parts = parts_of(which, *blocks[3 * which : 3 * which + 3], plus, minus)
        for slot, part in enumerate(parts):
            chip = chip_at(z, sign, slot)
            for l in range(LEVELS):
                upper = table[row + l][:1]
                value = jnp.where(upper > 0, part[2 * l + 1].astype(jnp.float32), part[2 * l].astype(jnp.float32))
                out[which, l, chip] = value.astype(jnp.bfloat16)


def last_kernel(entries, table, sums, side, other_side, mine, got, average, params, momentum, *outs):
    path_out, momentum_out, params_out = outs
    core = lax.axis_index("core")
    total = jnp.sum(sums[...] + side[...] + other_side[...], axis=1, keepdims=True)
    factor = jnp.minimum(1.0, CLIP_RMS / jnp.sqrt(total / entries + EPSILON_SQ))
    row = lax.broadcasted_iota(jnp.int32, factor.shape, 0)
    for k in range(LEVELS // STEPS):
        l = pl.program_id(0) * (LEVELS // STEPS) + k
        low, high = (jnp.sum(jnp.where(row == 2 * l + m, factor, 0.0), axis=0, keepdims=True) for m in range(2))
        for m, scale in enumerate((low, high)):
            at = 2 * k + m
            skipped = table[SKIPPED + 2 * l + m][:1] > 0
            clipped = scale * average[at]
            before, old = momentum[at], params[at]
            after = jnp.where(skipped, before, MOMENTUM_COEF * before + clipped)
            momentum_out[at] = after
            params_out[at] = jnp.where(skipped, old, old - OUTER_RATE * (clipped + MOMENTUM_COEF * after))
        upper = table[OWN_UPPER + l][:1] > 0
        scale = CLIPPED_COEF * jnp.where(upper, high, low)
        for half, part in ((core, mine), (1 - core, got)):
            for block in range(CHIPS):
                at = pl.ds(pl.multiple_of((2 * block + half) * BLOCK, BLOCK), BLOCK)
                new = part[1, l, block].astype(jnp.float32) - scale * part[0, l, block].astype(jnp.float32)
                path_out[k, :, at] = new.astype(jnp.bfloat16)


def cost(bytes_accessed):
    return pl.CostEstimate(flops=0, bytes_accessed=bytes_accessed, transcendentals=0)


def size_of(arrays):
    return sum(a.size * a.dtype.itemsize for a in arrays)


def call(kernel, outs, *args):
    shapes = [jax.ShapeDtypeStruct(s, d) for s, d in outs]
    return pl.pallas_call(
        kernel,
        out_shape=shapes,
        in_specs=[VMEM] * len(args),
        out_specs=[VMEM] * len(shapes),
        cost_estimate=cost(size_of(args) + size_of(shapes)),
        compiler_params=pltpu.CompilerParams(vmem_limit_bytes=24 * 2**20),
    )(*args)


def levelwise(kernel, outs, fixed, *args):
    shapes = [jax.ShapeDtypeStruct(s, d) for s, d in outs]

    def one(shape):
        return pl.BlockSpec((shape[0] // LEVELS, *shape[1:]), lambda l: (l, *[0] * (len(shape) - 1)))

    return pl.pallas_call(
        kernel,
        grid=(LEVELS,),
        out_shape=shapes,
        in_specs=[VMEM] * len(fixed) + [one(a.shape) for a in args],
        out_specs=[one(s.shape) for s in shapes],
        cost_estimate=cost(size_of(args) + size_of(shapes)),
        compiler_params=pltpu.CompilerParams(vmem_limit_bytes=24 * 2**20),
    )(*fixed, *args)


def last(entries, table, sums, side, other_side, mine, got, average, params, momentum):
    _, _, _, rows, _ = mine.shape
    outs = [
        jax.ShapeDtypeStruct((LEVELS, rows, 2 * CHIPS * BLOCK), jnp.bfloat16),
        *[jax.ShapeDtypeStruct(average.shape, jnp.float32)] * 2,
    ]

    def one(shape):
        return pl.BlockSpec((shape[0] // STEPS, *shape[1:]), lambda l: (l, *[0] * (len(shape) - 1)))

    return pl.pallas_call(
        lambda *refs: last_kernel(entries, *refs),
        grid=(STEPS,),
        out_shape=outs,
        in_specs=[
            *[VMEM] * 6,
            *[one(average.shape)] * 3,
        ],
        out_specs=[one(o.shape) for o in outs],
        cost_estimate=cost(size_of((mine, got, average, params, momentum)) + size_of(outs)),
        compiler_params=pltpu.CompilerParams(vmem_limit_bytes=24 * 2**20),
    )(table, sums, side, other_side, mine, got, average, params, momentum)


def given_half(routes, counts, flags, delta, feedback):
    _, rows, _ = delta.shape
    half = jax.ShapeDtypeStruct((LEVELS, CHIPS, rows, BLOCK), jnp.bfloat16)
    table = jax.ShapeDtypeStruct((TABLE, 8, BLOCK), jnp.float32)
    return pl.pallas_call(
        give_kernel,
        out_shape=[half, table],
        in_specs=[HBM] * 5,
        out_specs=[VMEM] * 2,
        scratch_shapes=[
            pltpu.SMEM(routes.shape, jnp.int32),
            pltpu.SMEM(counts.shape, jnp.int32),
            pltpu.SMEM(flags.shape, jnp.int32),
            pltpu.VMEM(delta.shape, delta.dtype),
            pltpu.VMEM(feedback.shape, feedback.dtype),
            pltpu.SemaphoreType.DMA((2, LEVELS)),
            pltpu.SemaphoreType.DMA((3,)),
        ],
        cost_estimate=cost(half.size * 16),
        compiler_params=pltpu.CompilerParams(vmem_limit_bytes=56 * 2**20),
    )(routes, counts, flags, delta, feedback)


def moved(x, up, down):
    def target(p):
        z, core = divmod(p, 2)
        return 2 * ((z + (down if core else up)) % CHIPS) + core

    return lax.ppermute(x, PATH, [(p, target(p)) for p in range(PATHS)])


def jump(x, steps):
    return moved(x, steps, -steps)


def swap(x):
    return lax.ppermute(x, "core", [(0, 1), (1, 0)])


def spread_far(x):
    return jump(x, 3), jump(x, -2)


def spread_near(*blocks):
    _, *tile = blocks[0].shape
    plus, minus = call(second_kernel, [((n * MODULES, *tile), blocks[0].dtype) for n in (4, 6)], *blocks)
    return *blocks, jump(plus, 1), jump(minus, -1)


def over_plane(x):
    parts = jnp.broadcast_to(x[None], (lax.axis_size(PLANE), *x.shape))
    return jnp.sum(lax.all_to_all(parts, PLANE, 0, 0), axis=0)


def on_device(path_delta, feedback, global_params, momentum, routes, token_counts, skip_flags):
    delta, feedback = path_delta[0], feedback[0]
    rows = delta.shape[1]
    params = global_params.reshape(MODULES, rows, BLOCK)
    momentum = momentum.reshape(MODULES, rows, BLOCK)
    f32, bf16 = jnp.float32, jnp.bfloat16
    half, block = (LEVELS, CHIPS, rows, BLOCK), (MODULES, rows, BLOCK)
    entries = rows * lax.axis_size(FSDP) * BLOCK * lax.axis_size(PATH)

    give, table = given_half(routes.T, token_counts.T, skip_flags.T, delta, feedback)
    got = swap(give)
    (keep,) = call(keep_kernel, [(half, bf16)], table, delta, feedback)
    plus, minus = call(outgoing_kernel, [((3, *block), bf16), ((2, *block), bf16)], table, keep, got)
    later, _ = lax.optimization_barrier((table, minus))
    plus, minus = jump(plus, 1), jump(minus, -1)
    (start,) = call(start_kernel, [(block, bf16)], later, params, momentum)
    later, _ = lax.optimization_barrier((later, start))
    (hold,) = call(staying_kernel, [((3, *block), bf16)], later, keep, got)
    (feedback_next,) = levelwise(feedback_kernel, [(delta.shape, f32)], (later,), delta, feedback)
    starts = start, *spread_far(start)
    hold, feedback_next = lax.optimization_barrier((hold, feedback_next))
    reduced_near = jump(hold[2] + plus[2], 2)
    reduced_far = jump(hold[1] + plus[1] + minus[1], -3)
    average, narrow = call(
        owner_kernel,
        [(block, f32), (block, bf16)],
        hold,
        plus,
        minus,
        reduced_near,
        reduced_far,
    )
    far, near = spread_far(narrow)
    spread = spread_near(narrow, far, near, *starts)
    (squares,) = call(squares_kernel, [((MODULES, 128), f32)], narrow, far, near)
    sums = over_plane(squares)
    later, sums = lax.optimization_barrier((table, sums))
    lane = lax.broadcasted_iota(jnp.int32, sums.shape, 1)
    side = jump(jnp.where(lane == 3 * lax.axis_index("core") + 2, 0.0, sums), 1)
    other_side = swap(side)

    def bound(kernel, value):
        return lambda *refs: kernel(value, *refs)

    chosen = [((2, *half), bf16)]
    (give,) = call(bound(select_kernel, SIBLING_UPPER), chosen, later, *spread)
    got = swap(give)
    (mine,) = call(bound(select_kernel, OWN_UPPER), chosen, later, *spread)
    path_params, momentum_next, params_next = last(
        entries, table, sums, side, other_side, mine, got, average, params, momentum
    )
    shape = global_params.shape
    return feedback_next[None], momentum_next.reshape(shape), params_next.reshape(shape), path_params[None]


def solution(mesh):
    finer = Mesh(mesh.devices.reshape(8, 2, 4, 4), (*PATH, *FSDP))
    by_path, by_column = P(PATH, None, FSDP, None), P(None, None, FSDP, PATH)
    return jax.shard_map(
        on_device,
        mesh=finer,
        in_specs=(by_path, by_path, by_column, by_column, P(), P(), P()),
        out_specs=(by_path, by_column, by_column, by_path),
        check_vma=False,
    )
```

```python
import jax
import jax.numpy as jnp
from jax import lax
from jax.experimental import pallas as pl
from jax.experimental.pallas import tpu as pltpu
from jax.sharding import Mesh
from jax.sharding import PartitionSpec as P

PATH = ("z", "core")
FSDP = ("y", "x")
PLANE = ("core", "y", "x")
CHIPS = 8
PATHS = 16
LEVELS = 4
MODULES = 8
BLOCK = 256
STEPS = 4

CLIP_RMS = 0.2
OUTER_RATE = 0.7
MOMENTUM_COEF = 0.9
EPSILON_SQ = 1e-06
CLIPPED_COEF = OUTER_RATE * (1.0 + MOMENTUM_COEF)
MOMENTUM_SHARE = OUTER_RATE * MOMENTUM_COEF * MOMENTUM_COEF

OWN_UPPER, SIBLING_UPPER, SKIPPED, WEIGHT, BACK, TABLE = 0, 4, 8, 16, 20, 24

VMEM = pl.BlockSpec(memory_space=pltpu.VMEM)
HBM = pl.BlockSpec(memory_space=pltpu.HBM)


def place():
    z, core = lax.axis_index("z"), lax.axis_index("core")
    return z, core, 1 - 2 * core


def chip_at(z, sign, steps):
    return (z + sign * steps) & (CHIPS - 1)


def send_half(weight, delta, feedback, half, out):
    for block in range(CHIPS):
        at = pl.ds(pl.multiple_of((2 * block + half) * BLOCK, BLOCK), BLOCK)
        corrected = delta[:, at].astype(jnp.float32) + feedback[:, at]
        out[block] = (weight * corrected).astype(jnp.bfloat16)


def give_kernel(routes_hbm, counts_hbm, flags_hbm, delta, feedback, give, table, *scratch):
    routes, counts, flags, delta_in, feedback_in, sems, table_sems = scratch
    _, rows, _ = delta.shape
    z, core, _ = place()
    path, sibling = 2 * z + core, 2 * z + 1 - core
    small = [
        pltpu.make_async_copy(src, dst, table_sems.at[i])
        for i, (src, dst) in enumerate(((routes_hbm, routes), (counts_hbm, counts), (flags_hbm, flags)))
    ]
    for copy in small:
        copy.start()
    copies = [
        (
            pltpu.make_async_copy(delta.at[l], delta_in.at[l], sems.at[0, l]),
            pltpu.make_async_copy(feedback.at[l], feedback_in.at[l], sems.at[1, l]),
        )
        for l in range(LEVELS)
    ]
    for pair in copies:
        for copy in pair:
            copy.start()
    for copy in small:
        copy.wait()
    tile = table.shape[1:]

    def splat(value):
        return jnp.full(tile, value, jnp.int32).astype(jnp.float32)

    for q in range(MODULES):
        table[SKIPPED + q] = splat(flags[q & 1, q >> 1])
    for l in range(LEVELS):
        own = routes[l, path]
        denom = jnp.int32(0)
        for p in range(PATHS):
            denom += jnp.where(routes[l, p] == own, counts[l, p], 0)
        top, bottom = splat(counts[l, path]), splat(denom)
        ratio = top / bottom
        high = ratio.astype(jnp.bfloat16).astype(jnp.float32)
        rest = (top - high * bottom) - (ratio - high) * bottom
        ratio = ratio + rest / bottom
        live = flags[own, l] == 0
        table[OWN_UPPER + l] = splat(own)
        table[SIBLING_UPPER + l] = splat(routes[l, sibling])
        table[WEIGHT + l] = ratio
        table[BACK + l] = jnp.where(live, bottom / top, 0.0)
        weight = jnp.where(live, ratio, 0.0)[:1]
        for copy in copies[l]:
            copy.wait()
        send_half(weight, delta_in.at[l], feedback_in.at[l], 1 - core, give.at[l])


def keep_kernel(table, delta, feedback, keep):
    core = lax.axis_index("core")
    for l in range(LEVELS):
        weight = jnp.where(table[BACK + l] > 0, table[WEIGHT + l], 0.0)[:1]
        send_half(weight, delta.at[l], feedback.at[l], core, keep.at[l])


def feedback_kernel(table, delta, feedback, out):
    l = pl.program_id(0)
    weight, back = table[WEIGHT + l][:1], table[BACK + l][:1]
    for block in range(2 * CHIPS):
        at = pl.ds(block * BLOCK, BLOCK)
        corrected = delta[0, :, at].astype(jnp.float32) + feedback[0, :, at]
        sent = (weight * corrected).astype(jnp.bfloat16).astype(jnp.float32)
        out[0, :, at] = corrected - sent * back


def write_pairs(table, keep, got, out, jumps):
    z, _, sign = place()
    for l in range(LEVELS):
        own, sibling = table[OWN_UPPER + l][:1], table[SIBLING_UPPER + l][:1]
        for slot, steps in enumerate(jumps):
            chip = chip_at(z, sign, steps)
            first, second = keep[l, chip].astype(jnp.float32), got[l, chip].astype(jnp.float32)
            upper = own * first + sibling * second
            lower = (1.0 - own) * first + (1.0 - sibling) * second
            out[slot, 2 * l] = lower.astype(jnp.bfloat16)
            out[slot, 2 * l + 1] = upper.astype(jnp.bfloat16)


def outgoing_kernel(table, keep, got, plus, minus):
    write_pairs(table, keep, got, plus, (1, -2, 3))
    write_pairs(table, keep, got, minus, (-1, -4))


def staying_kernel(table, keep, got, hold):
    write_pairs(table, keep, got, hold, (0, -3, 2))


def start_kernel(table, params, momentum, start):
    for q in range(MODULES):
        share = MOMENTUM_SHARE * (1.0 - table[SKIPPED + q][:1])
        start[q] = (params[q] - share * momentum[q]).astype(jnp.bfloat16)


def owner_kernel(hold, plus, minus, near, far, average, narrow):
    for q in range(MODULES):
        total = hold[0, q].astype(jnp.float32)
        for part in (plus[0, q], minus[0, q], near[q], far[q]):
            total += part.astype(jnp.float32)
        average[q] = total
        narrow[q] = total.astype(jnp.bfloat16)


def squares_kernel(own, far, near, out):
    lane = lax.broadcasted_iota(jnp.int32, (1, out.shape[1]), 1) - 3 * lax.axis_index("core")
    for q in range(MODULES):
        row = jnp.zeros(lane.shape, jnp.float32)
        for i, block in enumerate((own, far, near)):
            value = block[q].astype(jnp.float32)
            total = jnp.sum(jnp.sum(value * value, axis=0, keepdims=True), axis=1, keepdims=True)
            row = jnp.where(lane == i, total, row)
        out[q : q + 1] = row


def second_kernel(*refs):
    *blocks, plus, minus = refs
    for i, block in enumerate(blocks):
        which, kind = divmod(i, 3)
        for q in range(MODULES):
            value = block[q]
            minus[(3 * which + kind) * MODULES + q] = value
            if kind < 2:
                plus[(2 * which + kind) * MODULES + q] = value


def parts_of(which, own, far, near, plus, minus):
    def above(at):
        return plus.at[pl.ds((2 * which + at) * MODULES, MODULES)]

    def below(at):
        return minus.at[pl.ds((3 * which + at) * MODULES, MODULES)]

    return (own, below(0), near, below(2), above(1), far, below(1), above(0))


def select_kernel(row, table, *refs):
    z, _, sign = place()
    *blocks, plus, minus, out = refs
    for which in range(2):
        parts = parts_of(which, *blocks[3 * which : 3 * which + 3], plus, minus)
        for slot, part in enumerate(parts):
            chip = chip_at(z, sign, slot)
            for l in range(LEVELS):
                upper = table[row + l][:1]
                value = jnp.where(upper > 0, part[2 * l + 1].astype(jnp.float32), part[2 * l].astype(jnp.float32))
                out[which, l, chip] = value.astype(jnp.bfloat16)


def last_kernel(entries, table, sums, side, other_side, mine, got, average, params, momentum, *outs):
    path_out, momentum_out, params_out = outs
    core = lax.axis_index("core")
    total = jnp.sum(sums[...] + side[...] + other_side[...], axis=1, keepdims=True)
    factor = jnp.minimum(1.0, CLIP_RMS / jnp.sqrt(total / entries + EPSILON_SQ))
    row = lax.broadcasted_iota(jnp.int32, factor.shape, 0)
    for k in range(LEVELS // STEPS):
        l = pl.program_id(0) * (LEVELS // STEPS) + k
        low, high = (jnp.sum(jnp.where(row == 2 * l + m, factor, 0.0), axis=0, keepdims=True) for m in range(2))
        for m, scale in enumerate((low, high)):
            at = 2 * k + m
            skipped = table[SKIPPED + 2 * l + m][:1] > 0
            clipped = scale * average[at]
            before, old = momentum[at], params[at]
            after = jnp.where(skipped, before, MOMENTUM_COEF * before + clipped)
            momentum_out[at] = after
            params_out[at] = jnp.where(skipped, old, old - OUTER_RATE * (clipped + MOMENTUM_COEF * after))
        upper = table[OWN_UPPER + l][:1] > 0
        scale = CLIPPED_COEF * jnp.where(upper, high, low)
        for half, part in ((core, mine), (1 - core, got)):
            for block in range(CHIPS):
                at = pl.ds(pl.multiple_of((2 * block + half) * BLOCK, BLOCK), BLOCK)
                new = part[1, l, block].astype(jnp.float32) - scale * part[0, l, block].astype(jnp.float32)
                path_out[k, :, at] = new.astype(jnp.bfloat16)


def cost(bytes_accessed):
    return pl.CostEstimate(flops=0, bytes_accessed=bytes_accessed, transcendentals=0)


def size_of(arrays):
    return sum(a.size * a.dtype.itemsize for a in arrays)


def call(kernel, outs, *args):
    shapes = [jax.ShapeDtypeStruct(s, d) for s, d in outs]
    return pl.pallas_call(
        kernel,
        out_shape=shapes,
        in_specs=[VMEM] * len(args),
        out_specs=[VMEM] * len(shapes),
        cost_estimate=cost(size_of(args) + size_of(shapes)),
        compiler_params=pltpu.CompilerParams(vmem_limit_bytes=24 * 2**20),
    )(*args)


def levelwise(kernel, outs, fixed, *args):
    shapes = [jax.ShapeDtypeStruct(s, d) for s, d in outs]

    def one(shape):
        return pl.BlockSpec((shape[0] // LEVELS, *shape[1:]), lambda l: (l, *[0] * (len(shape) - 1)))

    return pl.pallas_call(
        kernel,
        grid=(LEVELS,),
        out_shape=shapes,
        in_specs=[VMEM] * len(fixed) + [one(a.shape) for a in args],
        out_specs=[one(s.shape) for s in shapes],
        cost_estimate=cost(size_of(args) + size_of(shapes)),
        compiler_params=pltpu.CompilerParams(vmem_limit_bytes=24 * 2**20),
    )(*fixed, *args)


def last(entries, table, sums, side, other_side, mine, got, average, params, momentum):
    _, _, _, rows, _ = mine.shape
    outs = [
        jax.ShapeDtypeStruct((LEVELS, rows, 2 * CHIPS * BLOCK), jnp.bfloat16),
        *[jax.ShapeDtypeStruct(average.shape, jnp.float32)] * 2,
    ]

    def one(shape):
        return pl.BlockSpec((shape[0] // STEPS, *shape[1:]), lambda l: (l, *[0] * (len(shape) - 1)))

    return pl.pallas_call(
        lambda *refs: last_kernel(entries, *refs),
        grid=(STEPS,),
        out_shape=outs,
        in_specs=[
            *[VMEM] * 6,
            *[one(average.shape)] * 3,
        ],
        out_specs=[one(o.shape) for o in outs],
        cost_estimate=cost(size_of((mine, got, average, params, momentum)) + size_of(outs)),
        compiler_params=pltpu.CompilerParams(vmem_limit_bytes=24 * 2**20),
    )(table, sums, side, other_side, mine, got, average, params, momentum)


def given_half(routes, counts, flags, delta, feedback):
    _, rows, _ = delta.shape
    half = jax.ShapeDtypeStruct((LEVELS, CHIPS, rows, BLOCK), jnp.bfloat16)
    table = jax.ShapeDtypeStruct((TABLE, 8, BLOCK), jnp.float32)
    return pl.pallas_call(
        give_kernel,
        out_shape=[half, table],
        in_specs=[HBM] * 5,
        out_specs=[VMEM] * 2,
        scratch_shapes=[
            pltpu.SMEM(routes.shape, jnp.int32),
            pltpu.SMEM(counts.shape, jnp.int32),
            pltpu.SMEM(flags.shape, jnp.int32),
            pltpu.VMEM(delta.shape, delta.dtype),
            pltpu.VMEM(feedback.shape, feedback.dtype),
            pltpu.SemaphoreType.DMA((2, LEVELS)),
            pltpu.SemaphoreType.DMA((3,)),
        ],
        cost_estimate=cost(half.size * 16),
        compiler_params=pltpu.CompilerParams(vmem_limit_bytes=56 * 2**20),
    )(routes, counts, flags, delta, feedback)


def moved(x, up, down):
    def target(p):
        z, core = divmod(p, 2)
        return 2 * ((z + (down if core else up)) % CHIPS) + core

    return lax.ppermute(x, PATH, [(p, target(p)) for p in range(PATHS)])


def jump(x, steps):
    return moved(x, steps, -steps)


def swap(x):
    return lax.ppermute(x, "core", [(0, 1), (1, 0)])


def spread_far(x):
    return jump(x, 3), jump(x, -2)


def spread_near(*blocks):
    _, *tile = blocks[0].shape
    plus, minus = call(second_kernel, [((n * MODULES, *tile), blocks[0].dtype) for n in (4, 6)], *blocks)
    return *blocks, jump(plus, 1), jump(minus, -1)


def over_plane(x):
    parts = jnp.broadcast_to(x[None], (lax.axis_size(PLANE), *x.shape))
    return jnp.sum(lax.all_to_all(parts, PLANE, 0, 0), axis=0)


def on_device(path_delta, feedback, global_params, momentum, routes, token_counts, skip_flags):
    delta, feedback = path_delta[0], feedback[0]
    rows = delta.shape[1]
    params = global_params.reshape(MODULES, rows, BLOCK)
    momentum = momentum.reshape(MODULES, rows, BLOCK)
    f32, bf16 = jnp.float32, jnp.bfloat16
    half, block = (LEVELS, CHIPS, rows, BLOCK), (MODULES, rows, BLOCK)
    entries = rows * lax.axis_size(FSDP) * BLOCK * lax.axis_size(PATH)

    give, table = given_half(routes.T, token_counts.T, skip_flags.T, delta, feedback)
    got = swap(give)
    (keep,) = call(keep_kernel, [(half, bf16)], table, delta, feedback)
    plus, minus = call(outgoing_kernel, [((3, *block), bf16), ((2, *block), bf16)], table, keep, got)
    later, _ = lax.optimization_barrier((table, minus))
    plus, minus = jump(plus, 1), jump(minus, -1)
    (start,) = call(start_kernel, [(block, bf16)], later, params, momentum)
    later, _ = lax.optimization_barrier((later, start))
    (hold,) = call(staying_kernel, [((3, *block), bf16)], later, keep, got)
    (feedback_next,) = levelwise(feedback_kernel, [(delta.shape, f32)], (later,), delta, feedback)
    starts = start, *spread_far(start)
    hold, feedback_next = lax.optimization_barrier((hold, feedback_next))
    reduced_near = jump(hold[2] + plus[2], 2)
    reduced_far = jump(hold[1] + plus[1] + minus[1], -3)
    average, narrow = call(
        owner_kernel,
        [(block, f32), (block, bf16)],
        hold,
        plus,
        minus,
        reduced_near,
        reduced_far,
    )
    far, near = spread_far(narrow)
    spread = spread_near(narrow, far, near, *starts)
    (squares,) = call(squares_kernel, [((MODULES, 128), f32)], narrow, far, near)
    sums = over_plane(squares)
    later, sums = lax.optimization_barrier((table, sums))
    lane = lax.broadcasted_iota(jnp.int32, sums.shape, 1)
    side = jump(jnp.where(lane == 3 * lax.axis_index("core") + 2, 0.0, sums), 1)
    other_side = swap(side)

    def bound(kernel, value):
        return lambda *refs: kernel(value, *refs)

    chosen = [((2, *half), bf16)]
    (give,) = call(bound(select_kernel, SIBLING_UPPER), chosen, later, *spread)
    got = jnp.stack([swap(give[0]), swap(give[1])])
    (mine,) = call(bound(select_kernel, OWN_UPPER), chosen, later, *spread)
    path_params, momentum_next, params_next = last(
        entries, table, sums, side, other_side, mine, got, average, params, momentum
    )
    shape = global_params.shape
    return feedback_next[None], momentum_next.reshape(shape), params_next.reshape(shape), path_params[None]


def solution(mesh):
    finer = Mesh(mesh.devices.reshape(8, 2, 4, 4), (*PATH, *FSDP))
    by_path, by_column = P(PATH, None, FSDP, None), P(None, None, FSDP, PATH)
    return jax.shard_map(
        on_device,
        mesh=finer,
        in_specs=(by_path, by_path, by_column, by_column, P(), P(), P()),
        out_specs=(by_path, by_column, by_column, by_path),
        check_vma=False,
    )
```
